512 devices in a mesh: row: 32 (over z, x), col: 16 (over y, core).
Axes of the slice: x: 4, y: 8, z: 8, core: 2. Of those that a mesh axis runs over, the one named last changes fastest.
Arguments:
- incoming_hidden: bfloat16 [16384, 2048], P('row', 'col'), may hold values from -6 to 6
- input_norm_weight: bfloat16 [1, 2048], P(None, 'col'), may hold values from 0.5 to 1.5
- query_key_value_weight: bfloat16 [3, 2048, 2048], P(None, 'row', 'col'), may hold values from -0.125 to 0.125
- query_key_value_bias: bfloat16 [3, 2048], P(None, 'col'), may hold values from -27 to 27
- output_weight: bfloat16 [2048, 2048], P('col', 'row'), may hold values from -0.125 to 0.125
- adapter_down_weight: bfloat16 [16, 2, 16, 2048], P('col'), may hold values from -0.125 to 0.125
- adapter_up_weight: bfloat16 [16, 2, 16, 2048], P(None, None, None, 'col'), may hold values from -1.5 to 1.5
- slot_of_adapter: int32 [16], replicated, may hold values from 0 to 15, each once
- adapter_of_prompt: int32 [32, 4], P('row'), may hold values from 0 to 15
- prompt_length_list: int32 [32, 4], P('row'), may hold values from 1 to 256, 512 in all within a row
- cache_page_index: int32 [32, 32], P('row'), may hold values from 0 to 31, each once within a row
Outputs:
- attn_out: bfloat16 [16384, 2048], P(('row', 'col'))
- kv_pages: bfloat16 [1024, 2, 16, 2048], P('row', None, None, 'col')
The draws below stay inside these ranges and needn't reach their ends.
All inputs are finite; a program needn't handle non-finite values.
Results may differ from the reference program's by a relative error of at most 0.023.
Values may be sent and summed in bfloat16 or wider, within the bound.
No kernel may reach another device: no remote copies, remote signals or barrier semaphores. Data moves between devices by JAX's collectives and lax.ppermute only.
A program may use at most 64 MiB of HBM per device.

```python
import math
import jax
import jax.numpy as jnp
import numpy as np
from jax import lax

MODEL_WIDTH = 2048
HEADS = 16
HEAD_DIM = 128
ADAPTER_RANK = 16
ADAPTER_SLOTS = 16
TOK_ROW = 512
SEQ_ROW = 4
PAGE = 16
MOST = 256
PAGES_ROW = 32
GROUPS = 32
TOKENS = 16384
N_COL = 16


def draw_query_key_value_bias(key, part):
    first = jax.random.fold_in(key, 0)
    drawn = jnp.clip(jax.random.normal(first, (3, MODEL_WIDTH), jnp.float32) * 0.5, -3.0, 3.0)
    return drawn.astype(jnp.bfloat16)


def set_ends(entries, rng, least, high):
    shape = entries.shape
    place = [jax.random.randint(jax.random.fold_in(rng, axis), (), 0, shape[axis]) for axis in range(len(shape))]
    entries = entries.at[tuple(place)].set(least)
    longest = shape.index(max(shape))
    place[longest] = (place[longest] + 1) % shape[longest]
    return entries.at[tuple(place)].set(high)


def block_scale(key, extent, pieces, low, top_value):
    loudness = 1.0
    for dim, parts in pieces:
        draws = jax.random.uniform(jax.random.fold_in(jax.random.fold_in(key, 6), dim), (parts,), jnp.float32, low / len(pieces), top_value / len(pieces))
        loudness = loudness * jnp.repeat(jnp.exp(draws), extent[dim] // parts).reshape((-1,) + (1,) * (len(extent) - 1 - dim))
    return loudness


def cumulative_ranks(count, skew):
    portions = [(1 << 20) // math.isqrt(grade ** skew) + 1 for grade in range(1, count + 1)]
    deviation = 1 + sum(portions) // (1 << 30)
    return np.cumsum(np.array([max(1, weight // deviation) for weight in portions]))


def ranked_ids(rng, extent, count, slope):
    listing = cumulative_ranks(count, slope)
    lot = jax.random.randint(jax.random.fold_in(rng, 1), extent, 0, int(listing[count - 1]))
    rank = jnp.searchsorted(jnp.asarray(listing, jnp.int32), lot, side="right")
    return jax.random.permutation(jax.random.fold_in(rng, 2), count)[rank].astype(jnp.int32)


def profile(count, total, most, lean):
    portions = [(1 << 20) // math.isqrt(grade ** lean) + 1 for grade in range(2, count + 1)]
    spare, holding = total - most - (count - 1), [1] * (count - 1)
    while spare > 0:
        candidates = [i for i in range(count - 1) if holding[i] < most]
        mass, remaining = sum([portions[i] for i in candidates]), spare
        for i in candidates:
            extra = min(most - holding[i], max(1, remaining * portions[i] // mass), spare)
            holding[i] = holding[i] + extra
            spare = spare - extra
    return np.array([most] + holding)


def ragged(rng, amount, total, bound, lean):
    if amount == 2:
        one = jax.random.randint(rng, (), max(1, total - bound), min(bound, total - 1) + 1)
        return jnp.stack([one, total - one])
    sizes = jnp.asarray(profile(amount, total, bound, lean), jnp.int32)
    pairs = (amount - 1) // 2
    source_of, sink = sizes[1:1 + 2 * pairs:2], sizes[2:2 + 2 * pairs:2]
    margin = jnp.minimum(source_of - 1, bound - sink)
    shifted = jax.random.randint(jax.random.fold_in(rng, 1), (pairs,), 0, 1 << 20) % (margin + 1)
    sizes = sizes.at[1:1 + 2 * pairs:2].set(source_of - shifted).at[2:2 + 2 * pairs:2].set(sink + shifted)
    return sizes[jax.random.permutation(jax.random.fold_in(rng, 2), amount)]


def scatter_about(key, extent, scale, bound, cuts=(), kind=jnp.bfloat16):
    array = jax.random.normal(key, extent, jnp.float32) * scale
    if len(cuts) > 0:
        array = block_scale(key, extent, cuts, -0.22, 0.18) * array
    return jnp.clip(array, min=-bound, max=bound).astype(kind)


def setup_inputs(seed: int = 0) -> dict:
    key_list = jax.random.split(jax.random.key(seed), 12)
    incoming_hidden = scatter_about(key_list[0], (TOKENS, MODEL_WIDTH), 1.0, 6.0, ((0, 32), (1, 16)))
    input_norm_weight = jnp.clip(0.5 + 1.0 * jax.random.uniform(key_list[1], (1, MODEL_WIDTH), jnp.float32) ** block_scale(key_list[1], (1, MODEL_WIDTH), ((1, 16),), -0.2, 0.2), 0.5, 1.5).astype(jnp.bfloat16)
    query_key_value_weight = scatter_about(key_list[2], (3, MODEL_WIDTH, MODEL_WIDTH), MODEL_WIDTH ** -0.5, 0.125, ((1, 32), (2, 16)))
    query_key_value_bias = draw_query_key_value_bias(jax.random.fold_in(key_list[11], 71), 0)
    output_weight = scatter_about(key_list[4], (MODEL_WIDTH, MODEL_WIDTH), MODEL_WIDTH ** -0.5, 0.125, ((0, 16), (1, 32)))
    adapter_down_weight = scatter_about(key_list[5], (ADAPTER_SLOTS, 2, ADAPTER_RANK, MODEL_WIDTH), MODEL_WIDTH ** -0.5, 0.125, ((0, 16),))
    adapter_up_weight = scatter_about(key_list[6], (ADAPTER_SLOTS, 2, ADAPTER_RANK, MODEL_WIDTH), ADAPTER_RANK ** -0.5, 1.5, ((3, 16),))
    slot_of_adapter = jax.random.permutation(key_list[7], ADAPTER_SLOTS).astype(jnp.int32)
    adapter_of_prompt = set_ends(ranked_ids(key_list[8], (GROUPS, SEQ_ROW), ADAPTER_SLOTS, 2), jax.random.fold_in(key_list[8], 3), 0, ADAPTER_SLOTS - 1).astype(jnp.int32)
    prompt_length_list = jax.vmap(lambda own: ragged(own, SEQ_ROW, TOK_ROW, MOST, 2))(jax.random.split(key_list[9], GROUPS)).reshape((GROUPS, SEQ_ROW)).astype(jnp.int32)
    cache_page_index = jax.vmap(lambda own: jax.random.permutation(own, PAGES_ROW))(jax.random.split(key_list[10], GROUPS)).reshape((GROUPS, PAGES_ROW)).astype(jnp.int32)
    return {"incoming_hidden": incoming_hidden, "input_norm_weight": input_norm_weight, "query_key_value_weight": query_key_value_weight, "query_key_value_bias": query_key_value_bias, "output_weight": output_weight, "adapter_down_weight": adapter_down_weight, "adapter_up_weight": adapter_up_weight, "slot_of_adapter": slot_of_adapter, "adapter_of_prompt": adapter_of_prompt, "prompt_length_list": prompt_length_list, "cache_page_index": cache_page_index}


rope_base = 1000000.0
norm_eps = 1e-06
adapter_scale = 2.0

def layout(lengths, total_rows):
    places = jnp.arange(total_rows, dtype=jnp.int32)
    prompt_end = jnp.cumsum(lengths).astype(jnp.int32)
    prompt_start = prompt_end - lengths
    inside = (places[:, None] >= prompt_start[None, :]) & (places[:, None] < prompt_end[None, :])
    numbers = jnp.arange(lengths.shape[0], dtype=jnp.int32)
    segment = lax.optimization_barrier(jnp.sum(jnp.where(inside, numbers[None, :], 0), axis=1)).astype(jnp.int32)
    position = places - lax.optimization_barrier(jnp.sum(jnp.where(inside, prompt_start[None, :], 0), axis=1)).astype(jnp.int32)
    return (segment, position, inside)

def rotary(vectors, position):
    half_dim = vectors.shape[-1] // 2
    inverse_freq = rope_base ** (-(jnp.arange(half_dim, dtype=jnp.float32) * 2.0 / vectors.shape[-1]))
    angles = position.astype(jnp.float32)[:, None] * inverse_freq[None, :]
    cosine = jnp.cos(angles)[:, None, :]
    sine_part = jnp.sin(angles)[:, None, :]
    first_half = vectors[..., :half_dim]
    second_half = vectors[..., half_dim:]
    return jnp.concatenate([first_half * cosine - second_half * sine_part, second_half * cosine + first_half * sine_part], axis=-1)

def reference(incoming_hidden, input_norm_weight, query_key_value_weight, query_key_value_bias, output_weight, adapter_down_weight, adapter_up_weight, slot_of_adapter, adapter_of_prompt, prompt_length_list, cache_page_index):
    weight_wide = query_key_value_weight.astype(jnp.float32)
    bias_wide = query_key_value_bias.astype(jnp.float32)
    flattened_down = adapter_down_weight.reshape(ADAPTER_SLOTS * 2 * ADAPTER_RANK, MODEL_WIDTH)
    query_up_weight = adapter_up_weight[:, 0].reshape(ADAPTER_SLOTS * ADAPTER_RANK, MODEL_WIDTH)
    value_up_weight = adapter_up_weight[:, 1].reshape(ADAPTER_SLOTS * ADAPTER_RANK, MODEL_WIDTH)
    out_groups = output_weight.astype(jnp.float32).reshape(N_COL, MODEL_WIDTH // N_COL, MODEL_WIDTH)
    gain_wide = input_norm_weight.astype(jnp.float32)

    def one_group(inputs):
        rows_in, lengths, adapters, table = inputs
        widened = rows_in.astype(jnp.float32)
        power = lax.optimization_barrier(jnp.mean(widened * widened, axis=1, keepdims=True))
        normed = (widened * lax.rsqrt(power + norm_eps) * gain_wide).astype(jnp.bfloat16)
        segment, position, inside = layout(lengths, TOK_ROW)
        slot_token = slot_of_adapter[adapters][segment]
        projected_rows = jnp.einsum('td,kdh->kth', normed.astype(jnp.float32), weight_wide) + bias_wide[:, None, :]
        lowrank = jnp.dot(normed, flattened_down.T, preferred_element_type=jnp.float32).astype(jnp.bfloat16)
        lowrank = lowrank.reshape(TOK_ROW, ADAPTER_SLOTS, 2, ADAPTER_RANK)
        chosen = slot_token[:, None] == jnp.arange(ADAPTER_SLOTS, dtype=jnp.int32)[None, :]
        picked = jnp.where(chosen[:, :, None, None], lowrank, jnp.zeros_like(lowrank))
        query_update = jnp.dot(picked[:, :, 0, :].reshape(TOK_ROW, ADAPTER_SLOTS * ADAPTER_RANK), query_up_weight, preferred_element_type=jnp.float32)
        value_update = jnp.dot(picked[:, :, 1, :].reshape(TOK_ROW, ADAPTER_SLOTS * ADAPTER_RANK), value_up_weight, preferred_element_type=jnp.float32)
        query_rows = projected_rows[0] + adapter_scale * query_update
        value_rows = projected_rows[2] + adapter_scale * value_update
        keys_wide = projected_rows[1]
        queries_rot = rotary(query_rows.reshape(TOK_ROW, HEADS, HEAD_DIM), position).astype(jnp.bfloat16)
        keys_rot = rotary(keys_wide.reshape(TOK_ROW, HEADS, HEAD_DIM), position).astype(jnp.bfloat16)
        values_rot = value_rows.astype(jnp.bfloat16).reshape(TOK_ROW, HEADS, HEAD_DIM)
        stacked = jnp.stack([keys_rot.reshape(PAGES_ROW, PAGE, MODEL_WIDTH), values_rot.reshape(PAGES_ROW, PAGE, MODEL_WIDTH)], axis=1)
        cache = jnp.zeros_like(stacked).at[table].set(stacked)
        scores = jnp.einsum('qhd,khd->hqk', queries_rot.astype(jnp.float32), keys_rot.astype(jnp.float32)) * HEAD_DIM ** (-0.5)
        places = jnp.arange(TOK_ROW, dtype=jnp.int32)
        allowed = (segment[:, None] == segment[None, :]) & (places[None, :] <= places[:, None])
        scores = jnp.where(allowed[None], scores, -1e+30)
        highest = lax.optimization_barrier(jnp.max(scores, axis=-1, keepdims=True))
        exps = jnp.exp(scores - highest)
        probs = (exps / lax.optimization_barrier(jnp.sum(exps, axis=-1, keepdims=True))).astype(jnp.bfloat16)
        attended = jnp.einsum('hqk,khd->qhd', probs.astype(jnp.float32), values_rot.astype(jnp.float32)).astype(jnp.bfloat16)
        grouped = attended.reshape(TOK_ROW, N_COL, MODEL_WIDTH // N_COL).astype(jnp.float32)
        terms = jnp.einsum('tgh,ghd->gtd', grouped, out_groups)
        rounded = lax.optimization_barrier(terms.astype(jnp.bfloat16))
        result = lax.optimization_barrier(jnp.sum(rounded.astype(jnp.float32), axis=0)).astype(jnp.bfloat16)
        return (result, cache)
    results, caches = lax.map(one_group, (incoming_hidden.reshape(GROUPS, TOK_ROW, MODEL_WIDTH), prompt_length_list, adapter_of_prompt, cache_page_index))
    return (results.reshape(TOKENS, MODEL_WIDTH), caches.reshape(GROUPS * PAGES_ROW, 2, PAGE, MODEL_WIDTH))
```

```python
import jax
import jax.numpy as jnp
from jax import lax
from jax.sharding import PartitionSpec as P

HEAD_DIM = 128
PAGE = 16
GAIN_ROWS = 16
X_SIZE = 4

rope_base = 1000000.0
norm_eps = 1e-06
adapter_scale = 2.0


def layout(lengths, total_rows):
    places = jnp.arange(total_rows, dtype=jnp.int32)
    prompt_end = jnp.cumsum(lengths)
    prompt_start = prompt_end - lengths
    inside = (places[:, None] >= prompt_start[None, :]) & (places[:, None] < prompt_end[None, :])
    numbers = jnp.arange(lengths.shape[0], dtype=jnp.int32)
    segment = jnp.sum(jnp.where(inside, numbers[None, :], 0), axis=1)
    position = places - jnp.sum(jnp.where(inside, prompt_start[None, :], 0), axis=1)
    return (segment, position, inside)


def rotary(vectors, position):
    half_dim = vectors.shape[-1] // 2
    inverse_freq = rope_base ** (
        -(jnp.arange(half_dim, dtype=jnp.float32) * 2.0 / vectors.shape[-1])
    )
    angles = position.astype(jnp.float32)[:, None] * inverse_freq[None, :]
    cosine = jnp.cos(angles)
    sine_part = jnp.sin(angles)
    first_half = vectors[..., :half_dim]
    second_half = vectors[..., half_dim:]
    return jnp.concatenate(
        [
            first_half * cosine - second_half * sine_part,
            second_half * cosine + first_half * sine_part,
        ],
        axis=-1,
    )


def attend(queries_rot, keys_rot, values_rot, segment):
    total_rows = queries_rot.shape[0]
    factor = queries_rot.shape[-1] ** (-0.5)
    index = jnp.arange(total_rows, dtype=jnp.int32)
    scores = jnp.einsum("qd,kd->qk", queries_rot, keys_rot, preferred_element_type=jnp.float32)
    scores = scores * factor
    allowed = (segment[:, None] == segment[None, :]) & (index[None, :] <= index[:, None])
    scores = jnp.where(allowed, scores, -1e30)
    highest = jnp.max(scores, axis=-1, keepdims=True)
    exps = jnp.exp(scores - highest)
    probs = (exps / jnp.sum(exps, axis=-1, keepdims=True)).astype(jnp.bfloat16)
    return jnp.dot(probs, values_rot, preferred_element_type=jnp.float32).astype(jnp.bfloat16)


def copies(block, count):
    return jnp.broadcast_to(block[None], (count,) + block.shape)


def make_body(n_row, n_col):
    n_z = n_row // X_SIZE
    x_groups = [[z * X_SIZE + x for x in range(X_SIZE)] for z in range(n_z)]
    z_groups = [[z * X_SIZE + x for z in range(n_z)] for x in range(X_SIZE)]
    pair_groups = [[i, i + 1] for i in range(0, n_col, 2)]
    y_groups = [list(range(core, n_col, 2)) for core in range(2)]

    def body(
        incoming_hidden,
        input_norm_weight,
        query_key_value_weight,
        query_key_value_bias,
        output_weight,
        adapter_down_weight,
        adapter_up_weight,
        slot_of_adapter,
        adapter_of_prompt,
        prompt_length_list,
        cache_page_index,
    ):
        total_rows, feature_part = incoming_hidden.shape
        rank2 = adapter_down_weight.shape[1] * adapter_down_weight.shape[2]
        width = adapter_down_weight.shape[3]
        row_part = query_key_value_weight.shape[1]
        head_cols = query_key_value_weight.shape[2]
        rank = adapter_down_weight.shape[2]
        down_block = (
            adapter_down_weight.reshape(rank2, n_col, feature_part)
            .transpose(1, 0, 2)
            .reshape(n_col * rank2, feature_part)
        )
        payload = jnp.concatenate(
            [
                incoming_hidden,
                down_block,
                jnp.broadcast_to(input_norm_weight, (GAIN_ROWS, feature_part)),
            ],
            axis=0,
        )
        gathered = lax.all_gather(payload, "col", axis=0, tiled=False)
        weight_block = jnp.concatenate(
            [query_key_value_weight[i] for i in range(3)] + [output_weight.T], axis=1
        )
        over_z = lax.all_to_all(
            copies(weight_block, n_z), "row", 0, 0, tiled=False, axis_index_groups=z_groups
        )
        over_x = lax.all_to_all(
            copies(over_z, X_SIZE), "row", 0, 0, tiled=False, axis_index_groups=x_groups
        )
        weights = over_x.transpose(1, 0, 2, 3).reshape(n_row * row_part, 4 * head_cols)

        gathered_hidden = (
            gathered[:, :total_rows].transpose(1, 0, 2).reshape(total_rows, width)
        )
        down_full = (
            gathered[:, total_rows : total_rows + n_col * rank2]
            .reshape(n_col, n_col, rank2, feature_part)
            .transpose(0, 2, 1, 3)
            .reshape(n_col * rank2, width)
        )
        gain_full = gathered[:, total_rows + n_col * rank2].reshape(1, width)

        widened = gathered_hidden.astype(jnp.float32)
        power = jnp.mean(widened * widened, axis=1, keepdims=True)
        normed = (widened * lax.rsqrt(power + norm_eps) * gain_full.astype(jnp.float32)).astype(
            jnp.bfloat16
        )
        segment, position, inside = layout(prompt_length_list[0], total_rows)
        slot_prompt = slot_of_adapter[adapter_of_prompt[0]]
        slot_token = jnp.sum(jnp.where(inside, slot_prompt[None, :], 0), axis=1)
        projected = jnp.dot(
            normed, weights[:, : 3 * head_cols], preferred_element_type=jnp.float32
        )
        projected = projected + query_key_value_bias.astype(jnp.float32).reshape(1, 3 * head_cols)
        lowrank = lax.dot_general(
            normed, down_full, (((1,), (1,)), ((), ())), preferred_element_type=jnp.float32
        ).astype(jnp.bfloat16)
        every_slot = adapter_up_weight.shape[0]
        lowrank = lowrank.reshape(total_rows, every_slot, 2, rank)
        chosen = slot_token[:, None] == jnp.arange(every_slot, dtype=jnp.int32)[None, :]
        picked = jnp.where(chosen[:, :, None, None], lowrank, jnp.zeros_like(lowrank))
        query_update = jnp.dot(
            picked[:, :, 0, :].reshape(total_rows, -1),
            adapter_up_weight[:, 0].reshape(-1, head_cols),
            preferred_element_type=jnp.float32,
        )
        value_update = jnp.dot(
            picked[:, :, 1, :].reshape(total_rows, -1),
            adapter_up_weight[:, 1].reshape(-1, head_cols),
            preferred_element_type=jnp.float32,
        )
        query_rows = projected[:, :head_cols] + adapter_scale * query_update
        key_rows = projected[:, head_cols : 2 * head_cols]
        value_rows = projected[:, 2 * head_cols :] + adapter_scale * value_update
        queries_rot = rotary(query_rows, position).astype(jnp.bfloat16)
        keys_rot = rotary(key_rows, position).astype(jnp.bfloat16)
        values_rot = value_rows.astype(jnp.bfloat16)
        pages_here = total_rows // PAGE
        stacked = jnp.stack(
            [
                keys_rot.reshape(pages_here, PAGE, head_cols),
                values_rot.reshape(pages_here, PAGE, head_cols),
            ],
            axis=1,
        )
        cache = jnp.zeros_like(stacked).at[cache_page_index[0]].set(stacked)
        attended = attend(queries_rot, keys_rot, values_rot, segment)
        partial = lax.dot_general(
            attended,
            weights[:, 3 * head_cols :],
            (((1,), (1,)), ((), ())),
            preferred_element_type=jnp.float32,
        ).astype(jnp.bfloat16)
        out_rows = total_rows // n_col
        by_core = partial.reshape(n_col // 2, 2, out_rows, width).transpose(1, 0, 2, 3)
        pair = lax.all_to_all(by_core, "col", 0, 0, tiled=False, axis_index_groups=pair_groups)
        pair_sum = (pair[0].astype(jnp.float32) + pair[1].astype(jnp.float32)).astype(jnp.bfloat16)
        terms = lax.all_to_all(pair_sum, "col", 0, 0, tiled=False, axis_index_groups=y_groups)
        summed = jnp.sum(terms.astype(jnp.float32), axis=0).astype(jnp.bfloat16)
        return (summed, cache)

    return body


def solution(mesh):
    in_specs = (
        P("row", "col"),
        P(None, "col"),
        P(None, "row", "col"),
        P(None, "col"),
        P("col", "row"),
        P("col", None, None, None),
        P(None, None, None, "col"),
        P(),
        P("row", None),
        P("row", None),
        P("row", None),
    )
    out_specs = (P(("row", "col"), None), P("row", None, None, "col"))
    body = make_body(mesh.shape["row"], mesh.shape["col"])
    return jax.shard_map(body, mesh=mesh, in_specs=in_specs, out_specs=out_specs, check_vma=False)
```

```python
import jax
import jax.numpy as jnp
from jax import lax
from jax.experimental import pallas as pl
from jax.experimental.pallas import tpu as pltpu
from jax.sharding import PartitionSpec as P

HEAD_DIM = 128
PAGE = 16
GAIN_ROWS = 16
X_SIZE = 4
LONGEST = 256
BLOCK = 128

rope_base = 1000000.0
norm_eps = 1e-06
adapter_scale = 2.0

VMEM = pltpu.MemorySpace.VMEM
SMEM = pltpu.MemorySpace.SMEM


def payload_kernel(hidden, gain, down, out):
    rows, part = hidden.shape
    rank2 = down.shape[0]
    out[0:rows, :] = hidden[...]
    for block in range(down.shape[1] // part):
        out[rows + block * rank2 : rows + (block + 1) * rank2, :] = down[
            :, block * part : (block + 1) * part
        ]
    wide = jnp.broadcast_to(gain[...].astype(jnp.float32), (GAIN_ROWS, part))
    out[out.shape[0] - GAIN_ROWS :, :] = wide.astype(jnp.bfloat16)


def weight_copies_kernel(qkv, out_weight_t, out):
    cols = qkv.shape[2]
    for copy in range(out.shape[0]):
        for i in range(3):
            out[copy, :, i * cols : (i + 1) * cols] = qkv[i]
        out[copy, :, 3 * cols :] = out_weight_t[...]


def block_kernel(
    slots,
    adapters,
    lengths,
    pages,
    x_place,
    gathered,
    piece_0,
    piece_1,
    piece_2,
    piece_3,
    bias,
    up,
    cosine,
    sine_part,
    out,
    cache,
    hidden,
    gain,
    down_raw,
    weights,
    normed,
    down,
    up_wide,
    keys,
    values,
    attended,
    sem_hidden,
    sem_gain,
    sem_down,
    sem_weight,
):
    n_col, total_rows, part = hidden.shape
    width = n_col * part
    n_prompts = down_raw.shape[0]
    rank2 = down_raw.shape[1] // n_col
    rank = rank2 // 2
    blocks = total_rows // BLOCK
    me = x_place[0]

    gain_copy = pltpu.make_async_copy(
        gathered.at[:, pl.ds(gathered.shape[1] - GAIN_ROWS, GAIN_ROWS)], gain, sem_gain.at[0]
    )
    gain_copy.start()
    hidden_copies = []
    for i in range(blocks):
        rows = pl.ds(i * BLOCK, BLOCK)
        hidden_copies.append(
            pltpu.make_async_copy(gathered.at[:, rows], hidden.at[:, rows], sem_hidden.at[i])
        )
        hidden_copies[i].start()
    prompt_slots = [slots[adapters[0, p]] for p in range(n_prompts)]
    down_copies = []
    for p in range(n_prompts):
        down_copies.append(
            pltpu.make_async_copy(
                gathered.at[prompt_slots[p], pl.ds(total_rows, n_col * rank2)],
                down_raw.at[p],
                sem_down.at[p],
            )
        )
        down_copies[p].start()
    weight_copies = []
    for k, piece in enumerate((piece_0, piece_1, piece_2, piece_3)):
        source = lax.rem(me + (X_SIZE - k), X_SIZE)
        weight_copies.append(
            pltpu.make_async_copy(piece, weights.at[:, source], sem_weight.at[k])
        )
        weight_copies[k].start()

    up_wide[...] = jnp.zeros_like(up_wide)
    for p in range(n_prompts):
        first = p * rank2
        up_wide[first : first + rank, 0:HEAD_DIM] = up[prompt_slots[p], 0]
        up_wide[first + rank : first + rank2, HEAD_DIM:] = up[prompt_slots[p], 1]

    gain_copy.wait()
    for i in range(blocks):
        hidden_copies[i].wait()
        rows = slice(i * BLOCK, (i + 1) * BLOCK)
        squares = jnp.zeros((BLOCK, part), jnp.float32)
        for c in range(n_col):
            piece = hidden[c, rows, :].astype(jnp.float32)
            squares = squares + piece * piece
        power = jnp.sum(squares, axis=1, keepdims=True) * (1.0 / width)
        scale = lax.rsqrt(power + norm_eps)
        for c in range(n_col):
            piece = hidden[c, rows, :].astype(jnp.float32)
            gain_row = gain[c, 0:1, :].astype(jnp.float32)
            normed[rows, c * part : (c + 1) * part] = (piece * scale * gain_row).astype(
                jnp.bfloat16
            )
    for p in range(n_prompts):
        down_copies[p].wait()
        for c in range(n_col):
            down[p * rank2 : (p + 1) * rank2, c * part : (c + 1) * part] = down_raw[
                p, c * rank2 : (c + 1) * rank2, :
            ]
    for k in range(X_SIZE):
        weight_copies[k].wait()

    tokens = normed[...]
    weight_qkv = weights[:, :, :, 0 : 3 * HEAD_DIM].reshape(width, 3 * HEAD_DIM)
    projected = jnp.dot(tokens, weight_qkv, preferred_element_type=jnp.float32)
    lowrank = lax.dot_general(
        tokens, down[...], (((1,), (1,)), ((), ())), preferred_element_type=jnp.float32
    ).astype(jnp.bfloat16)

    end_0 = lengths[0, 0]
    end_1 = end_0 + lengths[0, 1]
    end_2 = end_1 + lengths[0, 2]
    place = lax.broadcasted_iota(jnp.int32, (total_rows, n_prompts * rank2), 0)
    segment = (
        (place >= end_0).astype(jnp.int32)
        + (place >= end_1).astype(jnp.int32)
        + (place >= end_2).astype(jnp.int32)
    )
    lane = lax.broadcasted_iota(jnp.int32, (total_rows, n_prompts * rank2), 1)
    in_prompt = (lane >= segment * rank2) & (lane < segment * rank2 + rank2)
    picked = jnp.where(in_prompt, lowrank.astype(jnp.float32), 0.0).astype(jnp.bfloat16)
    update = jnp.dot(picked, up_wide[...], preferred_element_type=jnp.float32)

    bias_wide = bias[...].astype(jnp.float32)
    query_rows = projected[:, 0:HEAD_DIM] + bias_wide[0:1] + adapter_scale * update[:, 0:HEAD_DIM]
    key_rows = projected[:, HEAD_DIM : 2 * HEAD_DIM] + bias_wide[1:2]
    value_rows = (
        projected[:, 2 * HEAD_DIM :] + bias_wide[2:3] + adapter_scale * update[:, HEAD_DIM:]
    )
    cos_all = cosine[...]
    sin_all = sine_part[...]
    half = HEAD_DIM // 2
    queries = (query_rows * cos_all + pltpu.roll(query_rows, half, 1) * sin_all).astype(
        jnp.bfloat16
    )
    keys[...] = (key_rows * cos_all + pltpu.roll(key_rows, half, 1) * sin_all).astype(jnp.bfloat16)
    values[...] = value_rows.astype(jnp.bfloat16)
    for page in range(total_rows // PAGE):
        to = pages[0, page]
        cache[to, 0] = keys[page * PAGE : (page + 1) * PAGE, :]
        cache[to, 1] = values[page * PAGE : (page + 1) * PAGE, :]

    factor = HEAD_DIM ** (-0.5)
    reach = LONGEST // BLOCK
    for i in range(blocks):
        low = max(0, i - reach) * BLOCK
        high = (i + 1) * BLOCK
        query = queries[i * BLOCK : high, :]
        scores = lax.dot_general(
            query, keys[low:high, :], (((1,), (1,)), ((), ())), preferred_element_type=jnp.float32
        )
        query_place = i * BLOCK + lax.broadcasted_iota(jnp.int32, scores.shape, 0)
        key_place = low + lax.broadcasted_iota(jnp.int32, scores.shape, 1)
        start = jnp.where(
            query_place >= end_2,
            end_2,
            jnp.where(query_place >= end_1, end_1, jnp.where(query_place >= end_0, end_0, 0)),
        )
        allowed = (key_place <= query_place) & (key_place >= start)
        scores = jnp.where(allowed, scores * factor, -1e30)
        highest = jnp.max(scores, axis=1, keepdims=True)
        exps = jnp.exp(scores - highest)
        probs = (exps * (1.0 / jnp.sum(exps, axis=1, keepdims=True))).astype(jnp.bfloat16)
        attended[i * BLOCK : high, :] = jnp.dot(
            probs, values[low:high, :], preferred_element_type=jnp.float32
        ).astype(jnp.bfloat16)

    weight_out = weights[:, :, :, 3 * HEAD_DIM :].reshape(width, HEAD_DIM)
    partial = lax.dot_general(
        attended[...], weight_out, (((1,), (1,)), ((), ())), preferred_element_type=jnp.float32
    ).astype(jnp.bfloat16)
    out_rows = out.shape[2]
    for b in range(n_col):
        out[b % 2, b // 2] = partial[b * out_rows : (b + 1) * out_rows, :]


def make_body(n_row, n_col):
    n_z = n_row // X_SIZE
    z_groups = [[z * X_SIZE + x for z in range(n_z)] for x in range(X_SIZE)]
    pair_groups = [[i, i + 1] for i in range(0, n_col, 2)]
    y_groups = [list(range(core, n_col, 2)) for core in range(2)]

    def x_shift(step):
        return [
            (z * X_SIZE + x, z * X_SIZE + (x + step) % X_SIZE)
            for z in range(n_z)
            for x in range(X_SIZE)
        ]

    def body(
        incoming_hidden,
        input_norm_weight,
        query_key_value_weight,
        query_key_value_bias,
        output_weight,
        adapter_down_weight,
        adapter_up_weight,
        slot_of_adapter,
        adapter_of_prompt,
        prompt_length_list,
        cache_page_index,
    ):
        total_rows, part = incoming_hidden.shape
        rank2 = adapter_down_weight.shape[1] * adapter_down_weight.shape[2]
        width = adapter_down_weight.shape[3]
        row_part = query_key_value_weight.shape[1]
        head_cols = query_key_value_weight.shape[2]
        n_prompts = prompt_length_list.shape[1]
        out_rows = total_rows // n_col
        payload_rows = total_rows + n_col * rank2 + GAIN_ROWS
        payload = pl.pallas_call(
            payload_kernel,
            out_shape=jax.ShapeDtypeStruct((payload_rows, part), jnp.bfloat16),
            name="payload",
        )(incoming_hidden, input_norm_weight, adapter_down_weight.reshape(rank2, width))
        gathered = lax.all_gather(payload, "col", axis=0, tiled=False)
        copies = pl.pallas_call(
            weight_copies_kernel,
            out_shape=jax.ShapeDtypeStruct((n_z, row_part, 4 * head_cols), jnp.bfloat16),
            name="weight_copies",
        )(query_key_value_weight, output_weight.T)
        over_z = lax.all_to_all(copies, "row", 0, 0, tiled=False, axis_index_groups=z_groups)
        pieces = [over_z] + [lax.ppermute(over_z, "row", x_shift(k)) for k in range(1, X_SIZE)]

        lengths = prompt_length_list[0]
        places = jnp.arange(total_rows, dtype=jnp.int32)
        ends = jnp.cumsum(lengths)
        start = jnp.zeros_like(places)
        for p in range(n_prompts - 1):
            start = jnp.where(places >= ends[p], ends[p], start)
        position = (places - start).astype(jnp.float32)
        half = HEAD_DIM // 2
        inverse_freq = rope_base ** (-(jnp.arange(half, dtype=jnp.float32) * 2.0 / HEAD_DIM))
        angles = position[:, None] * inverse_freq[None, :]
        cos_half = jnp.cos(angles)
        sin_half = jnp.sin(angles)
        cosine = jnp.concatenate([cos_half, cos_half], axis=1)
        sine_part = jnp.concatenate([-sin_half, sin_half], axis=1)
        x_place = lax.rem(lax.axis_index("row"), X_SIZE).astype(jnp.int32).reshape(1)

        whole = pl.BlockSpec(memory_space=VMEM)
        scalar = pl.BlockSpec(memory_space=SMEM)
        raw = pl.BlockSpec(memory_space=pl.ANY)
        partial, cache = pl.pallas_call(
            block_kernel,
            out_shape=(
                jax.ShapeDtypeStruct((2, n_col // 2, out_rows, width), jnp.bfloat16),
                jax.ShapeDtypeStruct((total_rows // PAGE, 2, PAGE, head_cols), jnp.bfloat16),
            ),
            in_specs=[scalar] * 5 + [raw] * 5 + [whole] * 4,
            out_specs=(whole, whole),
            scratch_shapes=[
                pltpu.VMEM((n_col, total_rows, part), jnp.bfloat16),
                pltpu.VMEM((n_col, GAIN_ROWS, part), jnp.bfloat16),
                pltpu.VMEM((n_prompts, n_col * rank2, part), jnp.bfloat16),
                pltpu.VMEM((n_z, X_SIZE, row_part, 4 * head_cols), jnp.bfloat16),
                pltpu.VMEM((total_rows, width), jnp.bfloat16),
                pltpu.VMEM((n_prompts * rank2, width), jnp.bfloat16),
                pltpu.VMEM((n_prompts * rank2, 2 * head_cols), jnp.bfloat16),
                pltpu.VMEM((total_rows, head_cols), jnp.bfloat16),
                pltpu.VMEM((total_rows, head_cols), jnp.bfloat16),
                pltpu.VMEM((total_rows, head_cols), jnp.bfloat16),
                pltpu.SemaphoreType.DMA((total_rows // BLOCK,)),
                pltpu.SemaphoreType.DMA((1,)),
                pltpu.SemaphoreType.DMA((n_prompts,)),
                pltpu.SemaphoreType.DMA((X_SIZE,)),
            ],
            compiler_params=pltpu.CompilerParams(vmem_limit_bytes=48 * 1024 * 1024),
            name="attention_block",
        )(
            slot_of_adapter,
            adapter_of_prompt,
            prompt_length_list,
            cache_page_index,
            x_place,
            gathered,
            *pieces,
            query_key_value_bias,
            adapter_up_weight,
            cosine,
            sine_part,
        )
        pair = lax.all_to_all(partial, "col", 0, 0, tiled=False, axis_index_groups=pair_groups)
        pair_sum = (pair[0].astype(jnp.float32) + pair[1].astype(jnp.float32)).astype(jnp.bfloat16)
        terms = lax.all_to_all(pair_sum, "col", 0, 0, tiled=False, axis_index_groups=y_groups)
        summed = jnp.sum(terms.astype(jnp.float32), axis=0).astype(jnp.bfloat16)
        return (summed, cache)

    return body


def solution(mesh):
    in_specs = (
        P("row", "col"),
        P(None, "col"),
        P(None, "row", "col"),
        P(None, "col"),
        P("col", "row"),
        P("col", None, None, None),
        P(None, None, None, "col"),
        P(),
        P("row", None),
        P("row", None),
        P("row", None),
    )
    out_specs = (P(("row", "col"), None), P("row", None, None, "col"))
    body = make_body(mesh.shape["row"], mesh.shape["col"])
    return jax.shard_map(body, mesh=mesh, in_specs=in_specs, out_specs=out_specs, check_vma=False)
```

```python
import jax
import jax.numpy as jnp
import numpy as np
from jax import lax
from jax.experimental import pallas as pl
from jax.experimental.pallas import tpu as pltpu
from jax.sharding import PartitionSpec as P

HEAD_DIM = 128
PAGE = 16
GAIN_ROWS = 16
X_SIZE = 4
LONGEST = 256
BLOCK = 128

rope_base = 1000000.0
norm_eps = 1e-06
adapter_scale = 2.0

VMEM = pltpu.MemorySpace.VMEM
SMEM = pltpu.MemorySpace.SMEM
HBM = pltpu.MemorySpace.HBM


def payload_kernel(hidden, gain, down, out):
    rows, part = hidden.shape
    rank2 = down.shape[0]
    out[0:rows, :] = hidden[...]
    for block in range(down.shape[1] // part):
        out[rows + block * rank2 : rows + (block + 1) * rank2, :] = down[
            :, block * part : (block + 1) * part
        ]
    wide = jnp.broadcast_to(gain[...].astype(jnp.float32), (GAIN_ROWS, part))
    out[out.shape[0] - GAIN_ROWS :, :] = wide.astype(jnp.bfloat16)


def weight_copies_kernel(qkv, out_weight_t, out):
    cols = qkv.shape[2]
    for copy in range(out.shape[0]):
        for i in range(3):
            out[copy, :, i * cols : (i + 1) * cols] = qkv[i]
        out[copy, :, 3 * cols :] = out_weight_t[...]


def norm_kernel(
    slots,
    adapters,
    lengths,
    gathered,
    bias,
    up,
    cosine,
    sine_part,
    gained_x,
    row_scale,
    offset,
    cos_all,
    sin_all,
    hidden,
    gain,
    down_raw,
    down_x,
    up_wide,
    sem_hidden,
    sem_gain,
    sem_down,
):
    n_col, total_rows, part = hidden.shape
    width = n_col * part
    n_prompts = down_raw.shape[0]
    rank2 = down_raw.shape[1] // n_col
    rank = rank2 // 2
    blocks = total_rows // BLOCK

    gain_copy = pltpu.make_async_copy(
        gathered.at[:, pl.ds(gathered.shape[1] - GAIN_ROWS, GAIN_ROWS)], gain, sem_gain.at[0]
    )
    gain_copy.start()
    hidden_copies = []
    for i in range(blocks):
        rows = pl.ds(i * BLOCK, BLOCK)
        hidden_copies.append(
            pltpu.make_async_copy(gathered.at[:, rows], hidden.at[:, rows], sem_hidden.at[i])
        )
        hidden_copies[i].start()
    prompt_slots = [slots[adapters[0, p]] for p in range(n_prompts)]
    down_copies = []
    for p in range(n_prompts):
        down_copies.append(
            pltpu.make_async_copy(
                gathered.at[prompt_slots[p], pl.ds(total_rows, n_col * rank2)],
                down_raw.at[p],
                sem_down.at[p],
            )
        )
        down_copies[p].start()

    up_wide[...] = jnp.zeros_like(up_wide)
    for p in range(n_prompts):
        first = p * rank2
        up_wide[first : first + rank, 0:HEAD_DIM] = up[prompt_slots[p], 0]
        up_wide[first + rank : first + rank2, HEAD_DIM:] = up[prompt_slots[p], 1]

    end_0 = lengths[0, 0]
    end_1 = end_0 + lengths[0, 1]
    end_2 = end_1 + lengths[0, 2]
    place_wide = lax.broadcasted_iota(jnp.int32, (total_rows, HEAD_DIM), 0)
    lane_sign = jnp.where(
        lax.broadcasted_iota(jnp.int32, (1, HEAD_DIM), 1) < HEAD_DIM // 2, -1.0, 1.0
    )
    start_cos = jnp.ones((total_rows, HEAD_DIM), jnp.float32)
    start_sin = jnp.zeros((total_rows, HEAD_DIM), jnp.float32)
    for end in (end_0, end_1, end_2):
        after = place_wide >= end
        start_cos = jnp.where(after, cosine[pl.ds(end, 1), :], start_cos)
        start_sin = jnp.where(after, sine_part[pl.ds(end, 1), :], start_sin)
    cos_all[...] = cosine[...] * start_cos + sine_part[...] * start_sin
    sin_all[...] = (sine_part[...] * start_cos - cosine[...] * start_sin) * lane_sign

    def by_x(one, two):
        low_half = lax.broadcasted_iota(jnp.int32, one.shape, 1) < part // 2
        one_turned = pltpu.roll(one, part // 2, 1)
        two_turned = pltpu.roll(two, part // 2, 1)
        return (
            jnp.where(low_half, one, two_turned).astype(jnp.bfloat16),
            jnp.where(low_half, one_turned, two).astype(jnp.bfloat16),
        )

    for p in range(n_prompts):
        down_copies[p].wait()
        rows = slice(p * rank2, (p + 1) * rank2)
        for quad in range(n_col // 4):
            lanes = slice(quad * part, (quad + 1) * part)
            for pair in range(2):
                c = quad * 4 + pair
                one = down_raw[p, c * rank2 : (c + 1) * rank2, :].astype(jnp.float32)
                two = down_raw[p, (c + 2) * rank2 : (c + 3) * rank2, :].astype(jnp.float32)
                even, odd = by_x(one, two)
                down_x[2 * pair, rows, lanes] = even
                down_x[2 * pair + 1, rows, lanes] = odd

    gain_copy.wait()
    for i in range(blocks):
        hidden_copies[i].wait()
        rows = slice(i * BLOCK, (i + 1) * BLOCK)
        squares = jnp.zeros((BLOCK, part), jnp.float32)
        for quad in range(n_col // 4):
            lanes = slice(quad * part, (quad + 1) * part)
            for pair in range(2):
                c = quad * 4 + pair
                one = hidden[c, rows, :].astype(jnp.float32)
                two = hidden[c + 2, rows, :].astype(jnp.float32)
                squares = squares + one * one + two * two
                even, odd = by_x(
                    one * gain[c, 0:1, :].astype(jnp.float32),
                    two * gain[c + 2, 0:1, :].astype(jnp.float32),
                )
                gained_x[2 * pair, rows, lanes] = even
                gained_x[2 * pair + 1, rows, lanes] = odd
        power = jnp.sum(squares, axis=1, keepdims=True) * (1.0 / width)
        row_scale[rows, :] = jnp.broadcast_to(lax.rsqrt(power + norm_eps), (BLOCK, HEAD_DIM))

    unscaled = jnp.zeros((total_rows, n_prompts * rank2), jnp.float32)
    for x in range(X_SIZE):
        unscaled = unscaled + lax.dot_general(
            gained_x[x], down_x[x], (((1,), (1,)), ((), ())), preferred_element_type=jnp.float32
        )
    lowrank = (unscaled * row_scale[...]).astype(jnp.bfloat16)
    place = lax.broadcasted_iota(jnp.int32, (total_rows, n_prompts * rank2), 0)
    segment = (
        (place >= end_0).astype(jnp.int32)
        + (place >= end_1).astype(jnp.int32)
        + (place >= end_2).astype(jnp.int32)
    )
    lane = lax.broadcasted_iota(jnp.int32, (total_rows, n_prompts * rank2), 1)
    in_prompt = (lane >= segment * rank2) & (lane < segment * rank2 + rank2)
    picked = jnp.where(in_prompt, lowrank.astype(jnp.float32), 0.0).astype(jnp.bfloat16)
    update = jnp.dot(picked, up_wide[...], preferred_element_type=jnp.float32)
    bias_wide = bias[...].astype(jnp.float32)
    offset[:, 0:HEAD_DIM] = bias_wide[0:1] + adapter_scale * update[:, 0:HEAD_DIM]
    offset[:, HEAD_DIM : 2 * HEAD_DIM] = jnp.broadcast_to(bias_wide[1:2], (total_rows, HEAD_DIM))
    offset[:, 2 * HEAD_DIM :] = bias_wide[2:3] + adapter_scale * update[:, HEAD_DIM:]


def block_kernel(
    lengths,
    pages,
    x_place,
    piece_0,
    piece_1,
    piece_2,
    piece_3,
    gained_x,
    row_scale,
    offset,
    cosine,
    sine_part,
    attended,
    cache,
    keys,
    values,
):
    total_rows = gained_x.shape[1]
    inner = gained_x.shape[2]
    blocks = total_rows // BLOCK
    me = x_place[0]
    unscaled = jnp.zeros(offset.shape, jnp.float32)
    for k, piece in enumerate((piece_0, piece_1, piece_2, piece_3)):
        source = lax.rem(me + (X_SIZE - k), X_SIZE)
        unscaled = unscaled + jnp.dot(
            gained_x[source],
            piece[:, :, 0 : 3 * HEAD_DIM].reshape(inner, 3 * HEAD_DIM),
            preferred_element_type=jnp.float32,
        )
    scale = row_scale[...]
    query_rows = unscaled[:, 0:HEAD_DIM] * scale + offset[:, 0:HEAD_DIM]
    key_rows = unscaled[:, HEAD_DIM : 2 * HEAD_DIM] * scale + offset[:, HEAD_DIM : 2 * HEAD_DIM]
    value_rows = unscaled[:, 2 * HEAD_DIM :] * scale + offset[:, 2 * HEAD_DIM :]
    half = HEAD_DIM // 2
    cos_all = cosine[...]
    sin_all = sine_part[...]
    queries = (query_rows * cos_all + pltpu.roll(query_rows, half, 1) * sin_all).astype(
        jnp.bfloat16
    )
    keys[...] = (key_rows * cos_all + pltpu.roll(key_rows, half, 1) * sin_all).astype(jnp.bfloat16)
    values[...] = value_rows.astype(jnp.bfloat16)
    for page in range(total_rows // PAGE):
        to = pages[0, page]
        cache[to, 0] = keys[page * PAGE : (page + 1) * PAGE, :]
        cache[to, 1] = values[page * PAGE : (page + 1) * PAGE, :]

    end_0 = lengths[0, 0]
    end_1 = end_0 + lengths[0, 1]
    end_2 = end_1 + lengths[0, 2]
    factor = HEAD_DIM ** (-0.5)
    reach = LONGEST // BLOCK
    for i in range(blocks):
        low = max(0, i - reach) * BLOCK
        high = (i + 1) * BLOCK
        query = queries[i * BLOCK : high, :]
        scores = lax.dot_general(
            query, keys[low:high, :], (((1,), (1,)), ((), ())), preferred_element_type=jnp.float32
        )
        query_place = i * BLOCK + lax.broadcasted_iota(jnp.int32, scores.shape, 0)
        key_place = low + lax.broadcasted_iota(jnp.int32, scores.shape, 1)
        start = jnp.where(
            query_place >= end_2,
            end_2,
            jnp.where(query_place >= end_1, end_1, jnp.where(query_place >= end_0, end_0, 0)),
        )
        allowed = (key_place <= query_place) & (key_place >= start)
        scores = jnp.where(allowed, scores * factor, -1e30)
        highest = jnp.max(scores, axis=1, keepdims=True)
        exps = jnp.exp(scores - highest)
        probs = (exps * (1.0 / jnp.sum(exps, axis=1, keepdims=True))).astype(jnp.bfloat16)
        attended[i * BLOCK : high, :] = jnp.dot(
            probs, values[low:high, :], preferred_element_type=jnp.float32
        ).astype(jnp.bfloat16)


def output_kernel(
    x_place, piece_0, piece_1, piece_2, piece_3, attended, out, out_weights, sem
):
    me = x_place[0]
    copies = []
    for k, piece in enumerate((piece_0, piece_1, piece_2, piece_3)):
        source = lax.rem(me + (X_SIZE - k), X_SIZE)
        piece = piece.at[:, :, pl.ds(piece.shape[2] - HEAD_DIM, HEAD_DIM)]
        copies.append(pltpu.make_async_copy(piece, out_weights.at[:, source], sem.at[k]))
        copies[k].start()
    for k in range(X_SIZE):
        copies[k].wait()
    width = out.shape[3]
    weight_out = out_weights[...].reshape(width, HEAD_DIM)
    partial = lax.dot_general(
        attended[...], weight_out, (((1,), (1,)), ((), ())), preferred_element_type=jnp.float32
    ).astype(jnp.bfloat16)
    out_rows = out.shape[2]
    for b in range(2 * out.shape[1]):
        out[b % 2, b // 2] = partial[b * out_rows : (b + 1) * out_rows, :]


def rotary_tables(rows):
    half = HEAD_DIM // 2
    inverse_freq = np.float32(rope_base) ** (
        -(np.arange(half, dtype=np.float32) * np.float32(2.0) / np.float32(HEAD_DIM))
    )
    angles = (
        np.arange(rows, dtype=np.float32)[:, None] * inverse_freq.astype(np.float32)[None, :]
    ).astype(np.float64)
    cosine = np.concatenate([np.cos(angles)] * 2, axis=1).astype(np.float32)
    sine_part = np.concatenate([np.sin(angles)] * 2, axis=1).astype(np.float32)
    return jnp.asarray(cosine), jnp.asarray(sine_part)


def make_body(n_row, n_col):
    n_z = n_row // X_SIZE
    z_groups = [[z * X_SIZE + x for z in range(n_z)] for x in range(X_SIZE)]
    pair_groups = [[i, i + 1] for i in range(0, n_col, 2)]
    y_groups = [list(range(core, n_col, 2)) for core in range(2)]

    def x_shift(step):
        return [
            (z * X_SIZE + x, z * X_SIZE + (x + step) % X_SIZE)
            for z in range(n_z)
            for x in range(X_SIZE)
        ]

    def body(
        incoming_hidden,
        input_norm_weight,
        query_key_value_weight,
        query_key_value_bias,
        output_weight,
        adapter_down_weight,
        adapter_up_weight,
        slot_of_adapter,
        adapter_of_prompt,
        prompt_length_list,
        cache_page_index,
    ):
        total_rows, part = incoming_hidden.shape
        rank2 = adapter_down_weight.shape[1] * adapter_down_weight.shape[2]
        width = adapter_down_weight.shape[3]
        row_part = query_key_value_weight.shape[1]
        head_cols = query_key_value_weight.shape[2]
        n_prompts = prompt_length_list.shape[1]
        out_rows = total_rows // n_col
        payload_rows = total_rows + n_col * rank2 + GAIN_ROWS
        payload = pl.pallas_call(
            payload_kernel,
            out_shape=jax.ShapeDtypeStruct((payload_rows, part), jnp.bfloat16),
            name="payload",
        )(incoming_hidden, input_norm_weight, adapter_down_weight.reshape(rank2, width))
        gathered = lax.all_gather(payload, "col", axis=0, tiled=False)
        weight_copies = pl.pallas_call(
            weight_copies_kernel,
            out_shape=jax.ShapeDtypeStruct((n_z, row_part, 4 * head_cols), jnp.bfloat16),
            name="weight_copies",
        )(query_key_value_weight, output_weight.T)
        over_z = lax.all_to_all(weight_copies, "row", 0, 0, tiled=False, axis_index_groups=z_groups)
        own_qkv = over_z[:, :, : 3 * head_cols]
        own_out = over_z[:, :, 3 * head_cols :]
        pieces, out_pieces = [over_z] * X_SIZE, [over_z] * X_SIZE
        for k in (1, 3, 2):
            if k == 1:
                pieces[k] = out_pieces[k] = lax.ppermute(over_z, "row", x_shift(k))
            else:
                pieces[k] = lax.ppermute(own_qkv, "row", x_shift(k))
                out_pieces[k] = lax.ppermute(own_out, "row", x_shift(k))

        cosine, sine_part = rotary_tables(total_rows)
        x_place = lax.rem(lax.axis_index("row"), X_SIZE).astype(jnp.int32).reshape(1)

        whole = pl.BlockSpec(memory_space=VMEM)
        scalar = pl.BlockSpec(memory_space=SMEM)
        raw = pl.BlockSpec(memory_space=pl.ANY)
        gained_x, row_scale, offset, cos_all, sin_all = pl.pallas_call(
            norm_kernel,
            out_shape=(
                jax.ShapeDtypeStruct((X_SIZE, total_rows, width // X_SIZE), jnp.bfloat16),
                jax.ShapeDtypeStruct((total_rows, head_cols), jnp.float32),
                jax.ShapeDtypeStruct((total_rows, 3 * head_cols), jnp.float32),
                jax.ShapeDtypeStruct((total_rows, head_cols), jnp.float32),
                jax.ShapeDtypeStruct((total_rows, head_cols), jnp.float32),
            ),
            in_specs=[scalar] * 3 + [pl.BlockSpec(memory_space=HBM)] + [whole] * 4,
            out_specs=(whole,) * 5,
            scratch_shapes=[
                pltpu.VMEM((n_col, total_rows, part), jnp.bfloat16),
                pltpu.VMEM((n_col, GAIN_ROWS, part), jnp.bfloat16),
                pltpu.VMEM((n_prompts, n_col * rank2, part), jnp.bfloat16),
                pltpu.VMEM((X_SIZE, n_prompts * rank2, width // X_SIZE), jnp.bfloat16),
                pltpu.VMEM((n_prompts * rank2, 2 * head_cols), jnp.bfloat16),
                pltpu.SemaphoreType.DMA((total_rows // BLOCK,)),
                pltpu.SemaphoreType.DMA((1,)),
                pltpu.SemaphoreType.DMA((n_prompts,)),
            ],
            compiler_params=pltpu.CompilerParams(vmem_limit_bytes=32 * 1024 * 1024),
            name="norm_and_adapters",
        )(
            slot_of_adapter,
            adapter_of_prompt,
            prompt_length_list,
            pltpu.with_memory_space_constraint(gathered, HBM),
            query_key_value_bias,
            adapter_up_weight,
            cosine,
            sine_part,
        )
        attended, cache = pl.pallas_call(
            block_kernel,
            out_shape=(
                jax.ShapeDtypeStruct((total_rows, head_cols), jnp.bfloat16),
                jax.ShapeDtypeStruct((total_rows // PAGE, 2, PAGE, head_cols), jnp.bfloat16),
            ),
            in_specs=[scalar] * 3 + [whole] * 9,
            out_specs=(whole, whole),
            scratch_shapes=[
                pltpu.VMEM((total_rows, head_cols), jnp.bfloat16),
                pltpu.VMEM((total_rows, head_cols), jnp.bfloat16),
            ],
            compiler_params=pltpu.CompilerParams(vmem_limit_bytes=32 * 1024 * 1024),
            name="attention_block",
        )(
            prompt_length_list,
            cache_page_index,
            x_place,
            *pieces,
            gained_x,
            row_scale,
            offset,
            cos_all,
            sin_all,
        )
        partial = pl.pallas_call(
            output_kernel,
            out_shape=jax.ShapeDtypeStruct((2, n_col // 2, out_rows, width), jnp.bfloat16),
            in_specs=[scalar] + [raw] * X_SIZE + [whole],
            out_specs=whole,
            scratch_shapes=[
                pltpu.VMEM((n_z, X_SIZE, row_part, head_cols), jnp.bfloat16),
                pltpu.SemaphoreType.DMA((X_SIZE,)),
            ],
            compiler_params=pltpu.CompilerParams(vmem_limit_bytes=32 * 1024 * 1024),
            name="output_projection",
        )(x_place, *out_pieces, attended)
        pair = lax.all_to_all(partial, "col", 0, 0, tiled=False, axis_index_groups=pair_groups)
        pair_sum = (pair[0].astype(jnp.float32) + pair[1].astype(jnp.float32)).astype(jnp.bfloat16)
        terms = lax.all_to_all(pair_sum, "col", 0, 0, tiled=False, axis_index_groups=y_groups)
        summed = jnp.sum(terms.astype(jnp.float32), axis=0).astype(jnp.bfloat16)
        return (summed, cache)

    return body


def solution(mesh):
    in_specs = (
        P("row", "col"),
        P(None, "col"),
        P(None, "row", "col"),
        P(None, "col"),
        P("col", "row"),
        P("col", None, None, None),
        P(None, None, None, "col"),
        P(),
        P("row", None),
        P("row", None),
        P("row", None),
    )
    out_specs = (P(("row", "col"), None), P("row", None, None, "col"))
    body = make_body(mesh.shape["row"], mesh.shape["col"])
    return jax.shard_map(body, mesh=mesh, in_specs=in_specs, out_specs=out_specs, check_vma=False)
```

```python
import jax
import jax.numpy as jnp
import numpy as np
from jax import lax
from jax.experimental import pallas as pl
from jax.experimental.pallas import tpu as pltpu
from jax.sharding import PartitionSpec as P

HEAD_DIM = 128
PAGE = 16
GAIN_ROWS = 16
X_SIZE = 4
LONGEST = 256
BLOCK = 128

rope_base = 1000000.0
norm_eps = 1e-06
adapter_scale = 2.0

VMEM = pltpu.MemorySpace.VMEM
SMEM = pltpu.MemorySpace.SMEM
HBM = pltpu.MemorySpace.HBM


def outgoing_kernel(hidden, gain, down, qkv, out_weight_t, payload, copies):
    rows, part = hidden.shape
    rank2 = down.shape[0]
    payload[0:rows, :] = hidden[...]
    for block in range(down.shape[1] // part):
        payload[rows + block * rank2 : rows + (block + 1) * rank2, :] = down[
            :, block * part : (block + 1) * part
        ]
    wide = jnp.broadcast_to(gain[...].astype(jnp.float32), (GAIN_ROWS, part))
    payload[payload.shape[0] - GAIN_ROWS :, :] = wide.astype(jnp.bfloat16)
    cols = qkv.shape[2]
    for copy in range(copies.shape[0]):
        for i in range(3):
            copies[copy, :, i * cols : (i + 1) * cols] = qkv[i]
        copies[copy, :, 3 * cols :] = out_weight_t[...]


def norm_kernel(
    slots,
    adapters,
    lengths,
    gathered,
    bias,
    up,
    cosine,
    sine_part,
    gained_x,
    row_scale,
    offset,
    cos_all,
    sin_all,
    received,
    down_x,
    up_wide,
    in_prompt,
    sem_quad,
):
    n_col, received_rows, part = received.shape
    total_rows = row_scale.shape[0]
    width = n_col * part
    n_prompts = lengths.shape[1]
    rank2 = (received_rows - total_rows - GAIN_ROWS) // n_col
    rank = rank2 // 2
    gain_row = received_rows - GAIN_ROWS

    quads = n_col // 4
    quad_copies = []
    for q in range(quads):
        four = pl.ds(q * 4, 4)
        quad_copies.append(
            pltpu.make_async_copy(gathered.at[four], received.at[four], sem_quad.at[q])
        )
        quad_copies[q].start()
    prompt_slots = [slots[adapters[0, p]] for p in range(n_prompts)]

    up_wide[...] = jnp.zeros_like(up_wide)
    for p in range(n_prompts):
        first = p * rank2
        up_wide[first : first + rank, 0:HEAD_DIM] = up[prompt_slots[p], 0]
        up_wide[first + rank : first + rank2, HEAD_DIM:] = up[prompt_slots[p], 1]
    end_0 = lengths[0, 0]
    end_1 = end_0 + lengths[0, 1]
    end_2 = end_1 + lengths[0, 2]
    place = lax.broadcasted_iota(jnp.int32, (total_rows, HEAD_DIM), 0)
    lane = lax.broadcasted_iota(jnp.int32, (total_rows, HEAD_DIM), 1)
    lane_sign = jnp.where(lane[0:1] < HEAD_DIM // 2, -1.0, 1.0)
    start_cos = jnp.ones((total_rows, HEAD_DIM), jnp.float32)
    start_sin = jnp.zeros((total_rows, HEAD_DIM), jnp.float32)
    for end in (end_0, end_1, end_2):
        after = place >= end
        start_cos = jnp.where(after, cosine[pl.ds(end, 1), :], start_cos)
        start_sin = jnp.where(after, sine_part[pl.ds(end, 1), :], start_sin)
    cos_all[...] = cosine[...] * start_cos + sine_part[...] * start_sin
    sin_all[...] = (sine_part[...] * start_cos - cosine[...] * start_sin) * lane_sign
    segment = (
        (place >= end_0).astype(jnp.int32)
        + (place >= end_1).astype(jnp.int32)
        + (place >= end_2).astype(jnp.int32)
    )
    chosen = (lane >= segment * rank2) & (lane < segment * rank2 + rank2)
    in_prompt[...] = jnp.where(chosen, 1.0, 0.0)
    bias_wide = bias[...].astype(jnp.float32)
    offset[:, HEAD_DIM : 2 * HEAD_DIM] = jnp.broadcast_to(bias_wide[1:2], (total_rows, HEAD_DIM))

    def by_x(one, two):
        low_half = lax.broadcasted_iota(jnp.int32, one.shape, 1) < part // 2
        one_turned = pltpu.roll(one, part // 2, 1)
        two_turned = pltpu.roll(two, part // 2, 1)
        return (
            jnp.where(low_half, one, two_turned).astype(jnp.bfloat16),
            jnp.where(low_half, one_turned, two).astype(jnp.bfloat16),
        )

    for q in range(quads):
        quad_copies[q].wait()
        lanes = slice(q * part, (q + 1) * part)
        for pair in range(2):
            c = q * 4 + pair
            gain_one = received[c, gain_row : gain_row + 1, :].astype(jnp.float32)
            gain_two = received[c + 2, gain_row : gain_row + 1, :].astype(jnp.float32)
            for i in range(total_rows // BLOCK):
                rows = slice(i * BLOCK, (i + 1) * BLOCK)
                one = received[c, rows, :].astype(jnp.float32)
                two = received[c + 2, rows, :].astype(jnp.float32)
                squares = one * one + two * two
                row_scale[rows, :] = squares if c == 0 else row_scale[rows, :] + squares
                even, odd = by_x(one * gain_one, two * gain_two)
                gained_x[2 * pair, rows, lanes] = even
                gained_x[2 * pair + 1, rows, lanes] = odd
    for p in range(n_prompts):
        ranks = slice(p * rank2, (p + 1) * rank2)
        for q in range(quads):
            lanes = slice(q * part, (q + 1) * part)
            for pair in range(2):
                first = total_rows + (q * 4 + pair) * rank2
                second = first + 2 * rank2
                one = received[prompt_slots[p], first : first + rank2, :]
                two = received[prompt_slots[p], second : second + rank2, :]
                even, odd = by_x(one.astype(jnp.float32), two.astype(jnp.float32))
                down_x[2 * pair, ranks, lanes] = even
                down_x[2 * pair + 1, ranks, lanes] = odd
    power = jnp.sum(row_scale[...], axis=1, keepdims=True) * (1.0 / width)
    row_scale[...] = jnp.broadcast_to(lax.rsqrt(power + norm_eps), (total_rows, HEAD_DIM))
    unscaled = jnp.zeros((total_rows, n_prompts * rank2), jnp.float32)
    for x in range(X_SIZE):
        unscaled = unscaled + lax.dot_general(
            gained_x[x], down_x[x], (((1,), (1,)), ((), ())), preferred_element_type=jnp.float32
        )
    lowrank = (unscaled * row_scale[...]).astype(jnp.bfloat16)
    picked = (lowrank.astype(jnp.float32) * in_prompt[...]).astype(jnp.bfloat16)
    update = jnp.dot(picked, up_wide[...], preferred_element_type=jnp.float32)
    offset[:, 0:HEAD_DIM] = bias_wide[0:1] + adapter_scale * update[:, 0:HEAD_DIM]
    offset[:, 2 * HEAD_DIM :] = bias_wide[2:3] + adapter_scale * update[:, HEAD_DIM:]


def block_kernel(
    lengths,
    pages,
    x_place,
    piece_0,
    piece_1,
    piece_2,
    piece_3,
    gained_x,
    row_scale,
    offset,
    cosine,
    sine_part,
    attended,
    cache,
    keys,
    values,
):
    total_rows = gained_x.shape[1]
    inner = gained_x.shape[2]
    blocks = total_rows // BLOCK
    me = x_place[0]
    unscaled = jnp.zeros(offset.shape, jnp.float32)
    for k, piece in enumerate((piece_0, piece_1, piece_2, piece_3)):
        source = lax.rem(me + (X_SIZE - k), X_SIZE)
        unscaled = unscaled + jnp.dot(
            gained_x[source],
            piece[:, :, 0 : 3 * HEAD_DIM].reshape(inner, 3 * HEAD_DIM),
            preferred_element_type=jnp.float32,
        )
    scale = row_scale[...]
    query_rows = unscaled[:, 0:HEAD_DIM] * scale + offset[:, 0:HEAD_DIM]
    key_rows = unscaled[:, HEAD_DIM : 2 * HEAD_DIM] * scale + offset[:, HEAD_DIM : 2 * HEAD_DIM]
    value_rows = unscaled[:, 2 * HEAD_DIM :] * scale + offset[:, 2 * HEAD_DIM :]
    half = HEAD_DIM // 2
    cos_all = cosine[...]
    sin_all = sine_part[...]
    queries = (query_rows * cos_all + pltpu.roll(query_rows, half, 1) * sin_all).astype(
        jnp.bfloat16
    )
    keys[...] = (key_rows * cos_all + pltpu.roll(key_rows, half, 1) * sin_all).astype(jnp.bfloat16)
    values[...] = value_rows.astype(jnp.bfloat16)
    for page in range(total_rows // PAGE):
        to = pages[0, page]
        cache[to, 0] = keys[page * PAGE : (page + 1) * PAGE, :]
        cache[to, 1] = values[page * PAGE : (page + 1) * PAGE, :]

    end_0 = lengths[0, 0]
    end_1 = end_0 + lengths[0, 1]
    end_2 = end_1 + lengths[0, 2]
    factor = HEAD_DIM ** (-0.5)
    reach = LONGEST // BLOCK
    for i in range(blocks):
        low = max(0, i - reach) * BLOCK
        high = (i + 1) * BLOCK
        query = queries[i * BLOCK : high, :]
        scores = lax.dot_general(
            query, keys[low:high, :], (((1,), (1,)), ((), ())), preferred_element_type=jnp.float32
        )
        query_place = i * BLOCK + lax.broadcasted_iota(jnp.int32, scores.shape, 0)
        key_place = low + lax.broadcasted_iota(jnp.int32, scores.shape, 1)
        start = jnp.where(
            query_place >= end_2,
            end_2,
            jnp.where(query_place >= end_1, end_1, jnp.where(query_place >= end_0, end_0, 0)),
        )
        allowed = (key_place <= query_place) & (key_place >= start)
        scores = jnp.where(allowed, scores * factor, -1e30)
        highest = jnp.max(scores, axis=1, keepdims=True)
        exps = jnp.exp(scores - highest)
        probs = (exps * (1.0 / jnp.sum(exps, axis=1, keepdims=True))).astype(jnp.bfloat16)
        attended[i * BLOCK : high, :] = jnp.dot(
            probs, values[low:high, :], preferred_element_type=jnp.float32
        ).astype(jnp.bfloat16)


def output_kernel(
    x_place, piece_0, piece_1, piece_2, piece_3, attended, out, out_weights, sem
):
    me = x_place[0]
    copies = []
    for k, piece in enumerate((piece_0, piece_1, piece_2, piece_3)):
        source = lax.rem(me + (X_SIZE - k), X_SIZE)
        piece = piece.at[:, :, pl.ds(piece.shape[2] - HEAD_DIM, HEAD_DIM)]
        copies.append(pltpu.make_async_copy(piece, out_weights.at[:, source], sem.at[k]))
        copies[k].start()
    for k in range(X_SIZE):
        copies[k].wait()
    width = out.shape[3]
    weight_out = out_weights[...].reshape(width, HEAD_DIM)
    partial = lax.dot_general(
        attended[...], weight_out, (((1,), (1,)), ((), ())), preferred_element_type=jnp.float32
    ).astype(jnp.bfloat16)
    out_rows = out.shape[2]
    for b in range(2 * out.shape[1]):
        out[b % 2, b // 2] = partial[b * out_rows : (b + 1) * out_rows, :]


def rotary_tables(rows):
    half = HEAD_DIM // 2
    inverse_freq = np.float32(rope_base) ** (
        -(np.arange(half, dtype=np.float32) * np.float32(2.0) / np.float32(HEAD_DIM))
    )
    angles = (
        np.arange(rows, dtype=np.float32)[:, None] * inverse_freq.astype(np.float32)[None, :]
    ).astype(np.float64)
    cosine = np.concatenate([np.cos(angles)] * 2, axis=1).astype(np.float32)
    sine_part = np.concatenate([np.sin(angles)] * 2, axis=1).astype(np.float32)
    return jnp.asarray(cosine), jnp.asarray(sine_part)


def make_body(n_row, n_col):
    n_z = n_row // X_SIZE
    z_groups = [[z * X_SIZE + x for z in range(n_z)] for x in range(X_SIZE)]
    pair_groups = [[i, i + 1] for i in range(0, n_col, 2)]
    y_groups = [list(range(core, n_col, 2)) for core in range(2)]

    def x_shift(step):
        return [
            (z * X_SIZE + x, z * X_SIZE + (x + step) % X_SIZE)
            for z in range(n_z)
            for x in range(X_SIZE)
        ]

    def body(
        incoming_hidden,
        input_norm_weight,
        query_key_value_weight,
        query_key_value_bias,
        output_weight,
        adapter_down_weight,
        adapter_up_weight,
        slot_of_adapter,
        adapter_of_prompt,
        prompt_length_list,
        cache_page_index,
    ):
        total_rows, part = incoming_hidden.shape
        rank2 = adapter_down_weight.shape[1] * adapter_down_weight.shape[2]
        width = adapter_down_weight.shape[3]
        row_part = query_key_value_weight.shape[1]
        head_cols = query_key_value_weight.shape[2]
        n_prompts = prompt_length_list.shape[1]
        out_rows = total_rows // n_col
        payload_rows = total_rows + n_col * rank2 + GAIN_ROWS
        payload, weight_copies = pl.pallas_call(
            outgoing_kernel,
            out_shape=(
                jax.ShapeDtypeStruct((payload_rows, part), jnp.bfloat16),
                jax.ShapeDtypeStruct((n_z, row_part, 4 * head_cols), jnp.bfloat16),
            ),
            name="outgoing",
        )(
            incoming_hidden,
            input_norm_weight,
            adapter_down_weight.reshape(rank2, width),
            query_key_value_weight,
            output_weight.T,
        )
        gathered = lax.all_gather(payload, "col", axis=0, tiled=False)
        over_z = lax.all_to_all(weight_copies, "row", 0, 0, tiled=False, axis_index_groups=z_groups)
        own_qkv = over_z[:, :, : 3 * head_cols]
        own_out = over_z[:, :, 3 * head_cols :]
        pieces, out_pieces = [over_z] * X_SIZE, [over_z] * X_SIZE
        for k in (2, 1, 3):
            if k == 2:
                pieces[k] = out_pieces[k] = lax.ppermute(over_z, "row", x_shift(k))
            else:
                pieces[k] = lax.ppermute(own_qkv, "row", x_shift(k))
                out_pieces[k] = lax.ppermute(own_out, "row", x_shift(k))

        cosine, sine_part = rotary_tables(total_rows)
        x_place = lax.rem(lax.axis_index("row"), X_SIZE).astype(jnp.int32).reshape(1)

        whole = pl.BlockSpec(memory_space=VMEM)
        scalar = pl.BlockSpec(memory_space=SMEM)
        raw = pl.BlockSpec(memory_space=pl.ANY)
        gained_x, row_scale, offset, cos_all, sin_all = pl.pallas_call(
            norm_kernel,
            out_shape=(
                jax.ShapeDtypeStruct((X_SIZE, total_rows, width // X_SIZE), jnp.bfloat16),
                jax.ShapeDtypeStruct((total_rows, head_cols), jnp.float32),
                jax.ShapeDtypeStruct((total_rows, 3 * head_cols), jnp.float32),
                jax.ShapeDtypeStruct((total_rows, head_cols), jnp.float32),
                jax.ShapeDtypeStruct((total_rows, head_cols), jnp.float32),
            ),
            in_specs=[scalar] * 3 + [pl.BlockSpec(memory_space=HBM)] + [whole] * 4,
            out_specs=(whole,) * 5,
            scratch_shapes=[
                pltpu.VMEM((n_col, payload_rows, part), jnp.bfloat16),
                pltpu.VMEM((X_SIZE, n_prompts * rank2, width // X_SIZE), jnp.bfloat16),
                pltpu.VMEM((n_prompts * rank2, 2 * head_cols), jnp.bfloat16),
                pltpu.VMEM((total_rows, n_prompts * rank2), jnp.float32),
                pltpu.SemaphoreType.DMA((n_col // 4,)),
            ],
            compiler_params=pltpu.CompilerParams(vmem_limit_bytes=32 * 1024 * 1024),
            name="norm_and_adapters",
        )(
            slot_of_adapter,
            adapter_of_prompt,
            prompt_length_list,
            pltpu.with_memory_space_constraint(gathered, HBM),
            query_key_value_bias,
            adapter_up_weight,
            cosine,
            sine_part,
        )
        attended, cache = pl.pallas_call(
            block_kernel,
            out_shape=(
                jax.ShapeDtypeStruct((total_rows, head_cols), jnp.bfloat16),
                jax.ShapeDtypeStruct((total_rows // PAGE, 2, PAGE, head_cols), jnp.bfloat16),
            ),
            in_specs=[scalar] * 3 + [whole] * 9,
            out_specs=(whole, whole),
            scratch_shapes=[
                pltpu.VMEM((total_rows, head_cols), jnp.bfloat16),
                pltpu.VMEM((total_rows, head_cols), jnp.bfloat16),
            ],
            compiler_params=pltpu.CompilerParams(vmem_limit_bytes=32 * 1024 * 1024),
            name="attention_block",
        )(
            prompt_length_list,
            cache_page_index,
            x_place,
            *pieces,
            gained_x,
            row_scale,
            offset,
            cos_all,
            sin_all,
        )
        partial = pl.pallas_call(
            output_kernel,
            out_shape=jax.ShapeDtypeStruct((2, n_col // 2, out_rows, width), jnp.bfloat16),
            in_specs=[scalar] + [raw] * X_SIZE + [whole],
            out_specs=whole,
            scratch_shapes=[
                pltpu.VMEM((n_z, X_SIZE, row_part, head_cols), jnp.bfloat16),
                pltpu.SemaphoreType.DMA((X_SIZE,)),
            ],
            compiler_params=pltpu.CompilerParams(vmem_limit_bytes=32 * 1024 * 1024),
            name="output_projection",
        )(x_place, *out_pieces, attended)
        pair = lax.all_to_all(partial, "col", 0, 0, tiled=False, axis_index_groups=pair_groups)
        pair_sum = (pair[0].astype(jnp.float32) + pair[1].astype(jnp.float32)).astype(jnp.bfloat16)
        terms = lax.all_to_all(pair_sum, "col", 0, 0, tiled=False, axis_index_groups=y_groups)
        summed = jnp.sum(terms.astype(jnp.float32), axis=0).astype(jnp.bfloat16)
        return (summed, cache)

    return body


def solution(mesh):
    in_specs = (
        P("row", "col"),
        P(None, "col"),
        P(None, "row", "col"),
        P(None, "col"),
        P("col", "row"),
        P("col", None, None, None),
        P(None, None, None, "col"),
        P(),
        P("row", None),
        P("row", None),
        P("row", None),
    )
    out_specs = (P(("row", "col"), None), P("row", None, None, "col"))
    body = make_body(mesh.shape["row"], mesh.shape["col"])
    return jax.shard_map(body, mesh=mesh, in_specs=in_specs, out_specs=out_specs, check_vma=False)
```

```python
import jax
import jax.numpy as jnp
import numpy as np
from jax import lax
from jax.experimental import pallas as pl
from jax.experimental.pallas import tpu as pltpu
from jax.sharding import PartitionSpec as P

HEAD_DIM = 128
PAGE = 16
GAIN_ROWS = 16
X_SIZE = 4
LONGEST = 256
BLOCK = 128
QUERY_ROWS = 256
LOG2_E = 1.4426950408889634

rope_base = 1000000.0
norm_eps = 1e-06
adapter_scale = 2.0

VMEM = pltpu.MemorySpace.VMEM
SMEM = pltpu.MemorySpace.SMEM
HBM = pltpu.MemorySpace.HBM


def outgoing_kernel(hidden, gain, down, qkv, out_weight_t, payload, copies):
    rows, part = hidden.shape
    rank2 = down.shape[0]
    payload[0:rows, :] = hidden[...]
    for block in range(down.shape[1] // part):
        payload[rows + block * rank2 : rows + (block + 1) * rank2, :] = down[
            :, block * part : (block + 1) * part
        ]
    wide = jnp.broadcast_to(gain[...].astype(jnp.float32), (GAIN_ROWS, part))
    payload[payload.shape[0] - GAIN_ROWS :, :] = wide.astype(jnp.bfloat16)
    cols = qkv.shape[2]
    for copy in range(copies.shape[0]):
        for i in range(3):
            copies[copy, :, i * cols : (i + 1) * cols] = qkv[i]
        copies[copy, :, 3 * cols :] = out_weight_t[...]


def norm_kernel(
    slots,
    adapters,
    lengths,
    gathered,
    bias,
    up,
    cosine,
    sine_part,
    gained_x,
    row_scale,
    offset,
    cos_all,
    sin_all,
    received,
    down_x,
    up_wide,
    in_prompt,
    sem_quad,
):
    n_col, received_rows, part = received.shape
    total_rows = row_scale.shape[0]
    width = n_col * part
    n_prompts = lengths.shape[1]
    rank2 = (received_rows - total_rows - GAIN_ROWS) // n_col
    rank = rank2 // 2
    gain_row = received_rows - GAIN_ROWS

    quads = n_col // 4
    quad_copies = []
    for q in range(quads):
        four = pl.ds(q * 4, 4)
        quad_copies.append(
            pltpu.make_async_copy(gathered.at[four], received.at[four], sem_quad.at[q])
        )
        quad_copies[q].start()
    prompt_slots = [slots[adapters[0, p]] for p in range(n_prompts)]

    up_wide[...] = jnp.zeros_like(up_wide)
    for p in range(n_prompts):
        first = p * rank2
        up_wide[first : first + rank, 0:HEAD_DIM] = up[prompt_slots[p], 0]
        up_wide[first + rank : first + rank2, HEAD_DIM:] = up[prompt_slots[p], 1]
    end_0 = lengths[0, 0]
    end_1 = end_0 + lengths[0, 1]
    end_2 = end_1 + lengths[0, 2]
    place = lax.broadcasted_iota(jnp.int32, (total_rows, HEAD_DIM), 0)
    lane = lax.broadcasted_iota(jnp.int32, (total_rows, HEAD_DIM), 1)
    lane_sign = jnp.where(lane[0:1] < HEAD_DIM // 2, -1.0, 1.0)
    start_cos = jnp.ones((total_rows, HEAD_DIM), jnp.float32)
    start_sin = jnp.zeros((total_rows, HEAD_DIM), jnp.float32)
    for end in (end_0, end_1, end_2):
        after = place >= end
        start_cos = jnp.where(after, cosine[pl.ds(end, 1), :], start_cos)
        start_sin = jnp.where(after, sine_part[pl.ds(end, 1), :], start_sin)
    cos_all[...] = cosine[...] * start_cos + sine_part[...] * start_sin
    sin_all[...] = (sine_part[...] * start_cos - cosine[...] * start_sin) * lane_sign
    segment = (
        (place >= end_0).astype(jnp.int32)
        + (place >= end_1).astype(jnp.int32)
        + (place >= end_2).astype(jnp.int32)
    )
    chosen = (lane >= segment * rank2) & (lane < segment * rank2 + rank2)
    in_prompt[...] = jnp.where(chosen, 1.0, 0.0)
    bias_wide = bias[...].astype(jnp.float32)
    offset[:, HEAD_DIM : 2 * HEAD_DIM] = jnp.broadcast_to(bias_wide[1:2], (total_rows, HEAD_DIM))

    def by_x(one, two):
        low_half = lax.broadcasted_iota(jnp.int32, one.shape, 1) < part // 2
        one_turned = pltpu.roll(one, part // 2, 1)
        two_turned = pltpu.roll(two, part // 2, 1)
        return (
            jnp.where(low_half, one, two_turned).astype(jnp.bfloat16),
            jnp.where(low_half, one_turned, two).astype(jnp.bfloat16),
        )

    for q in range(quads):
        quad_copies[q].wait()
        lanes = slice(q * part, (q + 1) * part)
        for pair in range(2):
            c = q * 4 + pair
            gain_one = received[c, gain_row : gain_row + 1, :].astype(jnp.float32)
            gain_two = received[c + 2, gain_row : gain_row + 1, :].astype(jnp.float32)
            for i in range(total_rows // BLOCK):
                rows = slice(i * BLOCK, (i + 1) * BLOCK)
                one = received[c, rows, :].astype(jnp.float32)
                two = received[c + 2, rows, :].astype(jnp.float32)
                squares = one * one + two * two
                row_scale[rows, :] = squares if c == 0 else row_scale[rows, :] + squares
                even, odd = by_x(one * gain_one, two * gain_two)
                gained_x[2 * pair, rows, lanes] = even
                gained_x[2 * pair + 1, rows, lanes] = odd
    for p in range(n_prompts):
        ranks = slice(p * rank2, (p + 1) * rank2)
        for q in range(quads):
            lanes = slice(q * part, (q + 1) * part)
            for pair in range(2):
                first = total_rows + (q * 4 + pair) * rank2
                second = first + 2 * rank2
                one = received[prompt_slots[p], first : first + rank2, :]
                two = received[prompt_slots[p], second : second + rank2, :]
                even, odd = by_x(one.astype(jnp.float32), two.astype(jnp.float32))
                down_x[2 * pair, ranks, lanes] = even
                down_x[2 * pair + 1, ranks, lanes] = odd
    power = jnp.sum(row_scale[...], axis=1, keepdims=True) * (1.0 / width)
    row_scale[...] = jnp.broadcast_to(lax.rsqrt(power + norm_eps), (total_rows, HEAD_DIM))
    unscaled = jnp.zeros((total_rows, n_prompts * rank2), jnp.float32)
    for x in range(X_SIZE):
        unscaled = unscaled + lax.dot_general(
            gained_x[x], down_x[x], (((1,), (1,)), ((), ())), preferred_element_type=jnp.float32
        )
    lowrank = (unscaled * row_scale[...]).astype(jnp.bfloat16)
    picked = (lowrank.astype(jnp.float32) * in_prompt[...]).astype(jnp.bfloat16)
    update = jnp.dot(picked, up_wide[...], preferred_element_type=jnp.float32)
    offset[:, 0:HEAD_DIM] = bias_wide[0:1] + adapter_scale * update[:, 0:HEAD_DIM]
    offset[:, 2 * HEAD_DIM :] = bias_wide[2:3] + adapter_scale * update[:, HEAD_DIM:]


def block_kernel(
    lengths,
    pages,
    x_place,
    piece_0,
    piece_1,
    piece_2,
    piece_3,
    gained_x,
    row_scale,
    offset,
    cosine,
    sine_part,
    attended,
    cache,
    keys,
    values,
):
    total_rows = gained_x.shape[1]
    inner = gained_x.shape[2]
    blocks = total_rows // QUERY_ROWS
    me = x_place[0]
    unscaled = jnp.zeros(offset.shape, jnp.float32)
    for k, piece in enumerate((piece_0, piece_1, piece_2, piece_3)):
        source = lax.rem(me + (X_SIZE - k), X_SIZE)
        unscaled = unscaled + jnp.dot(
            gained_x[source],
            piece[:, :, 0 : 3 * HEAD_DIM].reshape(inner, 3 * HEAD_DIM),
            preferred_element_type=jnp.float32,
        )
    scale = row_scale[...]
    query_rows = unscaled[:, 0:HEAD_DIM] * scale + offset[:, 0:HEAD_DIM]
    key_rows = unscaled[:, HEAD_DIM : 2 * HEAD_DIM] * scale + offset[:, HEAD_DIM : 2 * HEAD_DIM]
    value_rows = unscaled[:, 2 * HEAD_DIM :] * scale + offset[:, 2 * HEAD_DIM :]
    half = HEAD_DIM // 2
    cos_all = cosine[...]
    sin_all = sine_part[...]
    queries = (query_rows * cos_all + pltpu.roll(query_rows, half, 1) * sin_all).astype(
        jnp.bfloat16
    )
    keys[...] = (key_rows * cos_all + pltpu.roll(key_rows, half, 1) * sin_all).astype(jnp.bfloat16)
    values[...] = value_rows.astype(jnp.bfloat16)
    for page in range(total_rows // PAGE):
        to = pages[0, page]
        cache[to, 0] = keys[page * PAGE : (page + 1) * PAGE, :]
        cache[to, 1] = values[page * PAGE : (page + 1) * PAGE, :]

    end_0 = lengths[0, 0]
    end_1 = end_0 + lengths[0, 1]
    end_2 = end_1 + lengths[0, 2]
    factor = HEAD_DIM ** (-0.5) * LOG2_E
    reach = LONGEST // QUERY_ROWS
    for i in range(blocks):
        low = max(0, i - reach) * QUERY_ROWS
        high = (i + 1) * QUERY_ROWS
        query = queries[i * QUERY_ROWS : high, :]
        scores = lax.dot_general(
            query, keys[low:high, :], (((1,), (1,)), ((), ())), preferred_element_type=jnp.float32
        )
        query_place = i * QUERY_ROWS + lax.broadcasted_iota(jnp.int32, scores.shape, 0)
        key_place = low + lax.broadcasted_iota(jnp.int32, scores.shape, 1)
        start = jnp.where(
            query_place >= end_2,
            end_2,
            jnp.where(query_place >= end_1, end_1, jnp.where(query_place >= end_0, end_0, 0)),
        )
        allowed = (key_place <= query_place) & (key_place >= start)
        scores = jnp.where(allowed, scores, -1e30)
        highest = jnp.max(scores, axis=1, keepdims=True)
        exps = jnp.exp2((scores - highest) * factor)
        total = jnp.sum(exps, axis=1, keepdims=True)
        mixed = jnp.dot(
            exps.astype(jnp.bfloat16), values[low:high, :], preferred_element_type=jnp.float32
        )
        attended[i * QUERY_ROWS : high, :] = (mixed * (1.0 / total)).astype(jnp.bfloat16)


def output_kernel(
    x_place, piece_0, piece_1, piece_2, piece_3, attended, out, out_weights, sem
):
    me = x_place[0]
    copies = []
    for k, piece in enumerate((piece_0, piece_1, piece_2, piece_3)):
        source = lax.rem(me + (X_SIZE - k), X_SIZE)
        piece = piece.at[:, :, pl.ds(piece.shape[2] - HEAD_DIM, HEAD_DIM)]
        copies.append(pltpu.make_async_copy(piece, out_weights.at[:, source], sem.at[k]))
        copies[k].start()
    for k in range(X_SIZE):
        copies[k].wait()
    width = out.shape[3]
    weight_out = out_weights[...].reshape(width, HEAD_DIM)
    partial = lax.dot_general(
        attended[...], weight_out, (((1,), (1,)), ((), ())), preferred_element_type=jnp.float32
    ).astype(jnp.bfloat16)
    out_rows = out.shape[2]
    for b in range(2 * out.shape[1]):
        out[b % 2, b // 2] = partial[b * out_rows : (b + 1) * out_rows, :]


def rotary_tables(rows):
    half = HEAD_DIM // 2
    inverse_freq = np.float32(rope_base) ** (
        -(np.arange(half, dtype=np.float32) * np.float32(2.0) / np.float32(HEAD_DIM))
    )
    angles = (
        np.arange(rows, dtype=np.float32)[:, None] * inverse_freq.astype(np.float32)[None, :]
    ).astype(np.float64)
    cosine = np.concatenate([np.cos(angles)] * 2, axis=1).astype(np.float32)
    sine_part = np.concatenate([np.sin(angles)] * 2, axis=1).astype(np.float32)
    return jnp.asarray(cosine), jnp.asarray(sine_part)


def make_body(n_row, n_col):
    n_z = n_row // X_SIZE
    z_groups = [[z * X_SIZE + x for z in range(n_z)] for x in range(X_SIZE)]
    pair_groups = [[i, i + 1] for i in range(0, n_col, 2)]
    y_groups = [list(range(core, n_col, 2)) for core in range(2)]

    def x_shift(step):
        return [
            (z * X_SIZE + x, z * X_SIZE + (x + step) % X_SIZE)
            for z in range(n_z)
            for x in range(X_SIZE)
        ]

    def body(
        incoming_hidden,
        input_norm_weight,
        query_key_value_weight,
        query_key_value_bias,
        output_weight,
        adapter_down_weight,
        adapter_up_weight,
        slot_of_adapter,
        adapter_of_prompt,
        prompt_length_list,
        cache_page_index,
    ):
        total_rows, part = incoming_hidden.shape
        rank2 = adapter_down_weight.shape[1] * adapter_down_weight.shape[2]
        width = adapter_down_weight.shape[3]
        row_part = query_key_value_weight.shape[1]
        head_cols = query_key_value_weight.shape[2]
        n_prompts = prompt_length_list.shape[1]
        out_rows = total_rows // n_col
        payload_rows = total_rows + n_col * rank2 + GAIN_ROWS
        payload, weight_copies = pl.pallas_call(
            outgoing_kernel,
            out_shape=(
                jax.ShapeDtypeStruct((payload_rows, part), jnp.bfloat16),
                jax.ShapeDtypeStruct((n_z, row_part, 4 * head_cols), jnp.bfloat16),
            ),
            name="outgoing",
        )(
            incoming_hidden,
            input_norm_weight,
            adapter_down_weight.reshape(rank2, width),
            query_key_value_weight,
            output_weight.T,
        )
        gathered = lax.all_gather(payload, "col", axis=0, tiled=False)
        over_z = lax.all_to_all(weight_copies, "row", 0, 0, tiled=False, axis_index_groups=z_groups)
        own_qkv = over_z[:, :, : 3 * head_cols]
        own_out = over_z[:, :, 3 * head_cols :]
        pieces, out_pieces = [over_z] * X_SIZE, [over_z] * X_SIZE
        for k in (2, 1, 3):
            if k == 2:
                pieces[k] = out_pieces[k] = lax.ppermute(over_z, "row", x_shift(k))
            else:
                pieces[k] = lax.ppermute(own_qkv, "row", x_shift(k))
                out_pieces[k] = lax.ppermute(own_out, "row", x_shift(k))

        cosine, sine_part = rotary_tables(total_rows)
        x_place = lax.rem(lax.axis_index("row"), X_SIZE).astype(jnp.int32).reshape(1)

        whole = pl.BlockSpec(memory_space=VMEM)
        scalar = pl.BlockSpec(memory_space=SMEM)
        raw = pl.BlockSpec(memory_space=pl.ANY)
        gained_x, row_scale, offset, cos_all, sin_all = pl.pallas_call(
            norm_kernel,
            out_shape=(
                jax.ShapeDtypeStruct((X_SIZE, total_rows, width // X_SIZE), jnp.bfloat16),
                jax.ShapeDtypeStruct((total_rows, head_cols), jnp.float32),
                jax.ShapeDtypeStruct((total_rows, 3 * head_cols), jnp.float32),
                jax.ShapeDtypeStruct((total_rows, head_cols), jnp.float32),
                jax.ShapeDtypeStruct((total_rows, head_cols), jnp.float32),
            ),
            in_specs=[scalar] * 3 + [pl.BlockSpec(memory_space=HBM)] + [whole] * 4,
            out_specs=(whole,) * 5,
            scratch_shapes=[
                pltpu.VMEM((n_col, payload_rows, part), jnp.bfloat16),
                pltpu.VMEM((X_SIZE, n_prompts * rank2, width // X_SIZE), jnp.bfloat16),
                pltpu.VMEM((n_prompts * rank2, 2 * head_cols), jnp.bfloat16),
                pltpu.VMEM((total_rows, n_prompts * rank2), jnp.float32),
                pltpu.SemaphoreType.DMA((n_col // 4,)),
            ],
            compiler_params=pltpu.CompilerParams(vmem_limit_bytes=32 * 1024 * 1024),
            name="norm_and_adapters",
        )(
            slot_of_adapter,
            adapter_of_prompt,
            prompt_length_list,
            pltpu.with_memory_space_constraint(gathered, HBM),
            query_key_value_bias,
            adapter_up_weight,
            cosine,
            sine_part,
        )
        attended, cache = pl.pallas_call(
            block_kernel,
            out_shape=(
                jax.ShapeDtypeStruct((total_rows, head_cols), jnp.bfloat16),
                jax.ShapeDtypeStruct((total_rows // PAGE, 2, PAGE, head_cols), jnp.bfloat16),
            ),
            in_specs=[scalar] * 3 + [whole] * 9,
            out_specs=(whole, whole),
            scratch_shapes=[
                pltpu.VMEM((total_rows, head_cols), jnp.bfloat16),
                pltpu.VMEM((total_rows, head_cols), jnp.bfloat16),
            ],
            compiler_params=pltpu.CompilerParams(vmem_limit_bytes=32 * 1024 * 1024),
            name="attention_block",
        )(
            prompt_length_list,
            cache_page_index,
            x_place,
            *pieces,
            gained_x,
            row_scale,
            offset,
            cos_all,
            sin_all,
        )
        partial = pl.pallas_call(
            output_kernel,
            out_shape=jax.ShapeDtypeStruct((2, n_col // 2, out_rows, width), jnp.bfloat16),
            in_specs=[scalar] + [raw] * X_SIZE + [whole],
            out_specs=whole,
            scratch_shapes=[
                pltpu.VMEM((n_z, X_SIZE, row_part, head_cols), jnp.bfloat16),
                pltpu.SemaphoreType.DMA((X_SIZE,)),
            ],
            compiler_params=pltpu.CompilerParams(vmem_limit_bytes=32 * 1024 * 1024),
            name="output_projection",
        )(x_place, *out_pieces, attended)
        pair = lax.all_to_all(partial, "col", 0, 0, tiled=False, axis_index_groups=pair_groups)
        pair_sum = (pair[0].astype(jnp.float32) + pair[1].astype(jnp.float32)).astype(jnp.bfloat16)
        terms = lax.all_to_all(pair_sum, "col", 0, 0, tiled=False, axis_index_groups=y_groups)
        summed = jnp.sum(terms.astype(jnp.float32), axis=0).astype(jnp.bfloat16)
        return (summed, cache)

    return body


def solution(mesh):
    in_specs = (
        P("row", "col"),
        P(None, "col"),
        P(None, "row", "col"),
        P(None, "col"),
        P("col", "row"),
        P("col", None, None, None),
        P(None, None, None, "col"),
        P(),
        P("row", None),
        P("row", None),
        P("row", None),
    )
    out_specs = (P(("row", "col"), None), P("row", None, None, "col"))
    body = make_body(mesh.shape["row"], mesh.shape["col"])
    return jax.shard_map(body, mesh=mesh, in_specs=in_specs, out_specs=out_specs, check_vma=False)
```

```python
import jax
import jax.numpy as jnp
import numpy as np
from jax import lax
from jax.experimental import pallas as pl
from jax.experimental.pallas import tpu as pltpu
from jax.sharding import PartitionSpec as P

HEAD_DIM = 128
PAGE = 16
GAIN_ROWS = 16
X_SIZE = 4
LONGEST = 256
BLOCK = 128
QUERY_ROWS = 256
LOG2_E = 1.4426950408889634

rope_base = 1000000.0
norm_eps = 1e-06
adapter_scale = 2.0

VMEM = pltpu.MemorySpace.VMEM
SMEM = pltpu.MemorySpace.SMEM
HBM = pltpu.MemorySpace.HBM


def outgoing_kernel(hidden, gain, down, qkv, out_weight_t, payload, copies):
    rows, part = hidden.shape
    rank2 = down.shape[0]
    payload[0:rows, :] = hidden[...]
    for block in range(down.shape[1] // part):
        payload[rows + block * rank2 : rows + (block + 1) * rank2, :] = down[
            :, block * part : (block + 1) * part
        ]
    wide = jnp.broadcast_to(gain[...].astype(jnp.float32), (GAIN_ROWS, part))
    payload[payload.shape[0] - GAIN_ROWS :, :] = wide.astype(jnp.bfloat16)
    cols = qkv.shape[2]
    for copy in range(copies.shape[0]):
        for i in range(3):
            copies[copy, :, i * cols : (i + 1) * cols] = qkv[i]
        copies[copy, :, 3 * cols :] = out_weight_t[...]


def norm_kernel(
    slots,
    adapters,
    lengths,
    gathered,
    bias,
    up,
    cosine,
    sine_part,
    gained_x,
    row_scale,
    offset,
    cos_all,
    sin_all,
    received,
    down_x,
    up_wide,
    in_prompt,
    sem_quad,
):
    n_col, received_rows, part = received.shape
    total_rows = row_scale.shape[0]
    width = n_col * part
    n_prompts = lengths.shape[1]
    rank2 = (received_rows - total_rows - GAIN_ROWS) // n_col
    rank = rank2 // 2
    gain_row = received_rows - GAIN_ROWS

    quads = n_col // 4
    quad_copies = []
    for q in range(quads):
        four = pl.ds(q * 4, 4)
        quad_copies.append(
            pltpu.make_async_copy(gathered.at[four], received.at[four], sem_quad.at[q])
        )
        quad_copies[q].start()
    prompt_slots = [slots[adapters[0, p]] for p in range(n_prompts)]

    up_wide[...] = jnp.zeros_like(up_wide)
    for p in range(n_prompts):
        first = p * rank2
        up_wide[first : first + rank, 0:HEAD_DIM] = up[prompt_slots[p], 0]
        up_wide[first + rank : first + rank2, HEAD_DIM:] = up[prompt_slots[p], 1]
    end_0 = lengths[0, 0]
    end_1 = end_0 + lengths[0, 1]
    end_2 = end_1 + lengths[0, 2]
    place = lax.broadcasted_iota(jnp.int32, (total_rows, HEAD_DIM), 0)
    lane = lax.broadcasted_iota(jnp.int32, (total_rows, HEAD_DIM), 1)
    lane_sign = jnp.where(lane[0:1] < HEAD_DIM // 2, -1.0, 1.0)
    start_cos = jnp.ones((total_rows, HEAD_DIM), jnp.float32)
    start_sin = jnp.zeros((total_rows, HEAD_DIM), jnp.float32)
    for end in (end_0, end_1, end_2):
        after = place >= end
        start_cos = jnp.where(after, cosine[pl.ds(end, 1), :], start_cos)
        start_sin = jnp.where(after, sine_part[pl.ds(end, 1), :], start_sin)
    cos_all[...] = cosine[...] * start_cos + sine_part[...] * start_sin
    sin_all[...] = (sine_part[...] * start_cos - cosine[...] * start_sin) * lane_sign
    segment = (
        (place >= end_0).astype(jnp.int32)
        + (place >= end_1).astype(jnp.int32)
        + (place >= end_2).astype(jnp.int32)
    )
    chosen = (lane >= segment * rank2) & (lane < segment * rank2 + rank2)
    in_prompt[...] = jnp.where(chosen, 1.0, 0.0)
    bias_wide = bias[...].astype(jnp.float32)
    offset[:, HEAD_DIM : 2 * HEAD_DIM] = jnp.broadcast_to(bias_wide[1:2], (total_rows, HEAD_DIM))

    def by_x(one, two):
        low_half = lax.broadcasted_iota(jnp.int32, one.shape, 1) < part // 2
        one_turned = pltpu.roll(one, part // 2, 1)
        two_turned = pltpu.roll(two, part // 2, 1)
        return (
            jnp.where(low_half, one, two_turned).astype(jnp.bfloat16),
            jnp.where(low_half, one_turned, two).astype(jnp.bfloat16),
        )

    for q in range(quads):
        quad_copies[q].wait()
        lanes = slice(q * part, (q + 1) * part)
        for pair in range(2):
            c = q * 4 + pair
            gain_one = received[c, gain_row : gain_row + 1, :].astype(jnp.float32)
            gain_two = received[c + 2, gain_row : gain_row + 1, :].astype(jnp.float32)
            for i in range(total_rows // BLOCK):
                rows = slice(i * BLOCK, (i + 1) * BLOCK)
                one = received[c, rows, :].astype(jnp.float32)
                two = received[c + 2, rows, :].astype(jnp.float32)
                squares = one * one + two * two
                row_scale[rows, :] = squares if c == 0 else row_scale[rows, :] + squares
                even, odd = by_x(one * gain_one, two * gain_two)
                gained_x[2 * pair, rows, lanes] = even
                gained_x[2 * pair + 1, rows, lanes] = odd
    for p in range(n_prompts):
        ranks = slice(p * rank2, (p + 1) * rank2)
        for q in range(quads):
            lanes = slice(q * part, (q + 1) * part)
            for pair in range(2):
                first = total_rows + (q * 4 + pair) * rank2
                second = first + 2 * rank2
                one = received[prompt_slots[p], first : first + rank2, :]
                two = received[prompt_slots[p], second : second + rank2, :]
                even, odd = by_x(one.astype(jnp.float32), two.astype(jnp.float32))
                down_x[2 * pair, ranks, lanes] = even
                down_x[2 * pair + 1, ranks, lanes] = odd
    power = jnp.sum(row_scale[...], axis=1, keepdims=True) * (1.0 / width)
    row_scale[...] = jnp.broadcast_to(lax.rsqrt(power + norm_eps), (total_rows, HEAD_DIM))
    unscaled = jnp.zeros((total_rows, n_prompts * rank2), jnp.float32)
    for x in range(X_SIZE):
        unscaled = unscaled + lax.dot_general(
            gained_x[x], down_x[x], (((1,), (1,)), ((), ())), preferred_element_type=jnp.float32
        )
    lowrank = (unscaled * row_scale[...]).astype(jnp.bfloat16)
    picked = (lowrank.astype(jnp.float32) * in_prompt[...]).astype(jnp.bfloat16)
    update = jnp.dot(picked, up_wide[...], preferred_element_type=jnp.float32)
    offset[:, 0:HEAD_DIM] = bias_wide[0:1] + adapter_scale * update[:, 0:HEAD_DIM]
    offset[:, 2 * HEAD_DIM :] = bias_wide[2:3] + adapter_scale * update[:, HEAD_DIM:]


def block_kernel(
    lengths,
    pages,
    x_place,
    piece_0,
    piece_1,
    piece_2,
    piece_3,
    gained_x,
    row_scale,
    offset,
    cosine,
    sine_part,
    attended,
    cache,
    keys,
    values,
):
    total_rows = gained_x.shape[1]
    inner = gained_x.shape[2]
    blocks = total_rows // QUERY_ROWS
    me = x_place[0]
    unscaled = jnp.zeros(offset.shape, jnp.float32)
    for k, piece in enumerate((piece_0, piece_1, piece_2, piece_3)):
        source = lax.rem(me + (X_SIZE - k), X_SIZE)
        unscaled = unscaled + jnp.dot(
            gained_x[source],
            piece[:, :, 0 : 3 * HEAD_DIM].reshape(inner, 3 * HEAD_DIM),
            preferred_element_type=jnp.float32,
        )
    scale = row_scale[...]
    query_rows = unscaled[:, 0:HEAD_DIM] * scale + offset[:, 0:HEAD_DIM]
    key_rows = unscaled[:, HEAD_DIM : 2 * HEAD_DIM] * scale + offset[:, HEAD_DIM : 2 * HEAD_DIM]
    value_rows = unscaled[:, 2 * HEAD_DIM :] * scale + offset[:, 2 * HEAD_DIM :]
    half = HEAD_DIM // 2
    cos_all = cosine[...]
    sin_all = sine_part[...]
    queries = (query_rows * cos_all + pltpu.roll(query_rows, half, 1) * sin_all).astype(
        jnp.bfloat16
    )
    keys[...] = (key_rows * cos_all + pltpu.roll(key_rows, half, 1) * sin_all).astype(jnp.bfloat16)
    values[...] = value_rows.astype(jnp.bfloat16)
    for page in range(total_rows // PAGE):
        to = pages[0, page]
        cache[to, 0] = keys[page * PAGE : (page + 1) * PAGE, :]
        cache[to, 1] = values[page * PAGE : (page + 1) * PAGE, :]

    end_0 = lengths[0, 0]
    end_1 = end_0 + lengths[0, 1]
    end_2 = end_1 + lengths[0, 2]
    factor = HEAD_DIM ** (-0.5) * LOG2_E
    reach = LONGEST // QUERY_ROWS
    for i in range(blocks):
        low = max(0, i - reach) * QUERY_ROWS
        high = (i + 1) * QUERY_ROWS
        query = queries[i * QUERY_ROWS : high, :]
        scores = lax.dot_general(
            query, keys[low:high, :], (((1,), (1,)), ((), ())), preferred_element_type=jnp.float32
        )
        query_place = i * QUERY_ROWS + lax.broadcasted_iota(jnp.int32, scores.shape, 0)
        key_place = low + lax.broadcasted_iota(jnp.int32, scores.shape, 1)
        start = jnp.where(
            query_place >= end_2,
            end_2,
            jnp.where(query_place >= end_1, end_1, jnp.where(query_place >= end_0, end_0, 0)),
        )
        allowed = (key_place <= query_place) & (key_place >= start)
        scores = jnp.where(allowed, scores, -1e30)
        highest = jnp.max(scores, axis=1, keepdims=True)
        exps = jnp.exp2((scores - highest) * factor)
        total = jnp.sum(exps, axis=1, keepdims=True)
        mixed = jnp.dot(
            exps.astype(jnp.bfloat16), values[low:high, :], preferred_element_type=jnp.float32
        )
        attended[i * QUERY_ROWS : high, :] = (mixed * (1.0 / total)).astype(jnp.bfloat16)


def output_kernel(
    x_place, core, piece_0, piece_1, piece_2, piece_3, attended, keep, send, out_weights, sem
):
    me = x_place[0]
    copies = []
    for k, piece in enumerate((piece_0, piece_1, piece_2, piece_3)):
        source = lax.rem(me + (X_SIZE - k), X_SIZE)
        piece = piece.at[:, :, pl.ds(piece.shape[2] - HEAD_DIM, HEAD_DIM)]
        copies.append(pltpu.make_async_copy(piece, out_weights.at[:, source], sem.at[k]))
        copies[k].start()
    for k in range(X_SIZE):
        copies[k].wait()
    width = keep.shape[2]
    weight_out = out_weights[...].reshape(width, HEAD_DIM)
    partial = lax.dot_general(
        attended[...], weight_out, (((1,), (1,)), ((), ())), preferred_element_type=jnp.float32
    ).astype(jnp.bfloat16)
    out_rows = keep.shape[1]

    def store(even, odd):
        for y in range(keep.shape[0]):
            first = 2 * y * out_rows
            even[y] = partial[first : first + out_rows, :]
            odd[y] = partial[first + out_rows : first + 2 * out_rows, :]

    @pl.when(core[0] == 0)
    def _():
        store(keep, send)

    @pl.when(core[0] == 1)
    def _():
        store(send, keep)


def rotary_tables(rows):
    half = HEAD_DIM // 2
    inverse_freq = np.float32(rope_base) ** (
        -(np.arange(half, dtype=np.float32) * np.float32(2.0) / np.float32(HEAD_DIM))
    )
    angles = (
        np.arange(rows, dtype=np.float32)[:, None] * inverse_freq.astype(np.float32)[None, :]
    ).astype(np.float64)
    cosine = np.concatenate([np.cos(angles)] * 2, axis=1).astype(np.float32)
    sine_part = np.concatenate([np.sin(angles)] * 2, axis=1).astype(np.float32)
    return jnp.asarray(cosine), jnp.asarray(sine_part)


def make_body(n_row, n_col):
    n_z = n_row // X_SIZE
    z_groups = [[z * X_SIZE + x for z in range(n_z)] for x in range(X_SIZE)]
    y_groups = [list(range(core, n_col, 2)) for core in range(2)]

    def x_shift(step):
        return [
            (z * X_SIZE + x, z * X_SIZE + (x + step) % X_SIZE)
            for z in range(n_z)
            for x in range(X_SIZE)
        ]

    def body(
        incoming_hidden,
        input_norm_weight,
        query_key_value_weight,
        query_key_value_bias,
        output_weight,
        adapter_down_weight,
        adapter_up_weight,
        slot_of_adapter,
        adapter_of_prompt,
        prompt_length_list,
        cache_page_index,
    ):
        total_rows, part = incoming_hidden.shape
        rank2 = adapter_down_weight.shape[1] * adapter_down_weight.shape[2]
        width = adapter_down_weight.shape[3]
        row_part = query_key_value_weight.shape[1]
        head_cols = query_key_value_weight.shape[2]
        n_prompts = prompt_length_list.shape[1]
        out_rows = total_rows // n_col
        payload_rows = total_rows + n_col * rank2 + GAIN_ROWS
        payload, weight_copies = pl.pallas_call(
            outgoing_kernel,
            out_shape=(
                jax.ShapeDtypeStruct((payload_rows, part), jnp.bfloat16),
                jax.ShapeDtypeStruct((n_z, row_part, 4 * head_cols), jnp.bfloat16),
            ),
            name="outgoing",
        )(
            incoming_hidden,
            input_norm_weight,
            adapter_down_weight.reshape(rank2, width),
            query_key_value_weight,
            output_weight.T,
        )
        gathered = lax.all_gather(payload, "col", axis=0, tiled=False)
        over_z = lax.all_to_all(weight_copies, "row", 0, 0, tiled=False, axis_index_groups=z_groups)
        own_qkv = over_z[:, :, : 3 * head_cols]
        own_out = over_z[:, :, 3 * head_cols :]
        pieces, out_pieces = [over_z] * X_SIZE, [over_z] * X_SIZE
        for k in (2, 1, 3):
            if k == 2:
                pieces[k] = out_pieces[k] = lax.ppermute(over_z, "row", x_shift(k))
            else:
                pieces[k] = lax.ppermute(own_qkv, "row", x_shift(k))
                out_pieces[k] = lax.ppermute(own_out, "row", x_shift(k))

        cosine, sine_part = rotary_tables(total_rows)
        x_place = lax.rem(lax.axis_index("row"), X_SIZE).astype(jnp.int32).reshape(1)

        whole = pl.BlockSpec(memory_space=VMEM)
        scalar = pl.BlockSpec(memory_space=SMEM)
        raw = pl.BlockSpec(memory_space=pl.ANY)
        gained_x, row_scale, offset, cos_all, sin_all = pl.pallas_call(
            norm_kernel,
            out_shape=(
                jax.ShapeDtypeStruct((X_SIZE, total_rows, width // X_SIZE), jnp.bfloat16),
                jax.ShapeDtypeStruct((total_rows, head_cols), jnp.float32),
                jax.ShapeDtypeStruct((total_rows, 3 * head_cols), jnp.float32),
                jax.ShapeDtypeStruct((total_rows, head_cols), jnp.float32),
                jax.ShapeDtypeStruct((total_rows, head_cols), jnp.float32),
            ),
            in_specs=[scalar] * 3 + [pl.BlockSpec(memory_space=HBM)] + [whole] * 4,
            out_specs=(whole,) * 5,
            scratch_shapes=[
                pltpu.VMEM((n_col, payload_rows, part), jnp.bfloat16),
                pltpu.VMEM((X_SIZE, n_prompts * rank2, width // X_SIZE), jnp.bfloat16),
                pltpu.VMEM((n_prompts * rank2, 2 * head_cols), jnp.bfloat16),
                pltpu.VMEM((total_rows, n_prompts * rank2), jnp.float32),
                pltpu.SemaphoreType.DMA((n_col // 4,)),
            ],
            compiler_params=pltpu.CompilerParams(vmem_limit_bytes=32 * 1024 * 1024),
            name="norm_and_adapters",
        )(
            slot_of_adapter,
            adapter_of_prompt,
            prompt_length_list,
            pltpu.with_memory_space_constraint(gathered, HBM),
            query_key_value_bias,
            adapter_up_weight,
            cosine,
            sine_part,
        )
        attended, cache = pl.pallas_call(
            block_kernel,
            out_shape=(
                jax.ShapeDtypeStruct((total_rows, head_cols), jnp.bfloat16),
                jax.ShapeDtypeStruct((total_rows // PAGE, 2, PAGE, head_cols), jnp.bfloat16),
            ),
            in_specs=[scalar] * 3 + [whole] * 9,
            out_specs=(whole, whole),
            scratch_shapes=[
                pltpu.VMEM((total_rows, head_cols), jnp.bfloat16),
                pltpu.VMEM((total_rows, head_cols), jnp.bfloat16),
            ],
            compiler_params=pltpu.CompilerParams(vmem_limit_bytes=32 * 1024 * 1024),
            name="attention_block",
        )(
            prompt_length_list,
            cache_page_index,
            x_place,
            *pieces,
            gained_x,
            row_scale,
            offset,
            cos_all,
            sin_all,
        )
        core = lax.rem(lax.axis_index("col"), 2).astype(jnp.int32).reshape(1)
        half_shape = jax.ShapeDtypeStruct((n_col // 2, out_rows, width), jnp.bfloat16)
        keep, send = pl.pallas_call(
            output_kernel,
            out_shape=(half_shape, half_shape),
            in_specs=[scalar] * 2 + [raw] * X_SIZE + [whole],
            out_specs=(whole, whole),
            scratch_shapes=[
                pltpu.VMEM((n_z, X_SIZE, row_part, head_cols), jnp.bfloat16),
                pltpu.SemaphoreType.DMA((X_SIZE,)),
            ],
            compiler_params=pltpu.CompilerParams(vmem_limit_bytes=32 * 1024 * 1024),
            name="output_projection",
        )(x_place, core, *out_pieces, attended)
        received = lax.ppermute(send, "col", [(i, i ^ 1) for i in range(n_col)])
        pair_sum = (keep.astype(jnp.float32) + received.astype(jnp.float32)).astype(jnp.bfloat16)
        terms = lax.all_to_all(pair_sum, "col", 0, 0, tiled=False, axis_index_groups=y_groups)
        summed = jnp.sum(terms.astype(jnp.float32), axis=0).astype(jnp.bfloat16)
        return (summed, cache)

    return body


def solution(mesh):
    in_specs = (
        P("row", "col"),
        P(None, "col"),
        P(None, "row", "col"),
        P(None, "col"),
        P("col", "row"),
        P("col", None, None, None),
        P(None, None, None, "col"),
        P(),
        P("row", None),
        P("row", None),
        P("row", None),
    )
    out_specs = (P(("row", "col"), None), P("row", None, None, "col"))
    body = make_body(mesh.shape["row"], mesh.shape["col"])
    return jax.shard_map(body, mesh=mesh, in_specs=in_specs, out_specs=out_specs, check_vma=False)
```

```python
import jax
import jax.numpy as jnp
import numpy as np
from jax import lax
from jax.experimental import pallas as pl
from jax.experimental.pallas import tpu as pltpu
from jax.sharding import PartitionSpec as P

HEAD_DIM = 128
PAGE = 16
GAIN_ROWS = 16
X_SIZE = 4
LONGEST = 256
BLOCK = 128
QUERY_ROWS = 256
LOG2_E = 1.4426950408889634

rope_base = 1000000.0
norm_eps = 1e-06
adapter_scale = 2.0

VMEM = pltpu.MemorySpace.VMEM
SMEM = pltpu.MemorySpace.SMEM
HBM = pltpu.MemorySpace.HBM


def outgoing_kernel(hidden, gain, down, qkv, out_weight_t, payload, copies):
    rows, part = hidden.shape
    rank2 = down.shape[0]
    payload[0:rows, :] = hidden[...]
    for block in range(down.shape[1] // part):
        payload[rows + block * rank2 : rows + (block + 1) * rank2, :] = down[
            :, block * part : (block + 1) * part
        ]
    wide = jnp.broadcast_to(gain[...].astype(jnp.float32), (GAIN_ROWS, part))
    payload[payload.shape[0] - GAIN_ROWS :, :] = wide.astype(jnp.bfloat16)
    cols = qkv.shape[2]
    for copy in range(copies.shape[0]):
        for i in range(3):
            copies[copy, :, i * cols : (i + 1) * cols] = qkv[i]
        copies[copy, :, 3 * cols :] = out_weight_t[...]


def norm_kernel(
    slots,
    adapters,
    lengths,
    gathered,
    bias,
    up,
    cosine,
    sine_part,
    gained_x,
    row_scale,
    offset,
    cos_all,
    sin_all,
    received,
    down_x,
    up_wide,
    in_prompt,
    sem_quad,
):
    n_col, received_rows, part = received.shape
    total_rows = row_scale.shape[0]
    width = n_col * part
    n_prompts = lengths.shape[1]
    rank2 = (received_rows - total_rows - GAIN_ROWS) // n_col
    rank = rank2 // 2
    gain_row = received_rows - GAIN_ROWS

    quads = n_col // 4
    quad_copies = []
    for q in range(quads):
        four = pl.ds(q * 4, 4)
        quad_copies.append(
            pltpu.make_async_copy(gathered.at[four], received.at[four], sem_quad.at[q])
        )
        quad_copies[q].start()
    prompt_slots = [slots[adapters[0, p]] for p in range(n_prompts)]

    up_wide[...] = jnp.zeros_like(up_wide)
    for p in range(n_prompts):
        first = p * rank2
        up_wide[first : first + rank, 0:HEAD_DIM] = up[prompt_slots[p], 0]
        up_wide[first + rank : first + rank2, HEAD_DIM:] = up[prompt_slots[p], 1]
    end_0 = lengths[0, 0]
    end_1 = end_0 + lengths[0, 1]
    end_2 = end_1 + lengths[0, 2]
    place = lax.broadcasted_iota(jnp.int32, (total_rows, HEAD_DIM), 0)
    lane = lax.broadcasted_iota(jnp.int32, (total_rows, HEAD_DIM), 1)
    lane_sign = jnp.where(lane[0:1] < HEAD_DIM // 2, -1.0, 1.0)
    start_cos = jnp.ones((total_rows, HEAD_DIM), jnp.float32)
    start_sin = jnp.zeros((total_rows, HEAD_DIM), jnp.float32)
    for end in (end_0, end_1, end_2):
        after = place >= end
        start_cos = jnp.where(after, cosine[pl.ds(end, 1), :], start_cos)
        start_sin = jnp.where(after, sine_part[pl.ds(end, 1), :], start_sin)
    cos_all[...] = cosine[...] * start_cos + sine_part[...] * start_sin
    sin_all[...] = (sine_part[...] * start_cos - cosine[...] * start_sin) * lane_sign
    segment = (
        (place >= end_0).astype(jnp.int32)
        + (place >= end_1).astype(jnp.int32)
        + (place >= end_2).astype(jnp.int32)
    )
    chosen = (lane >= segment * rank2) & (lane < segment * rank2 + rank2)
    in_prompt[...] = jnp.where(chosen, 1.0, 0.0)
    bias_wide = bias[...].astype(jnp.float32)
    offset[:, HEAD_DIM : 2 * HEAD_DIM] = jnp.broadcast_to(bias_wide[1:2], (total_rows, HEAD_DIM))

    def by_x(one, two):
        low_half = lax.broadcasted_iota(jnp.int32, one.shape, 1) < part // 2
        one_turned = pltpu.roll(one, part // 2, 1)
        two_turned = pltpu.roll(two, part // 2, 1)
        return (
            jnp.where(low_half, one, two_turned).astype(jnp.bfloat16),
            jnp.where(low_half, one_turned, two).astype(jnp.bfloat16),
        )

    for q in range(quads):
        quad_copies[q].wait()
        lanes = slice(q * part, (q + 1) * part)
        for pair in range(2):
            c = q * 4 + pair
            gain_one = received[c, gain_row : gain_row + 1, :].astype(jnp.float32)
            gain_two = received[c + 2, gain_row : gain_row + 1, :].astype(jnp.float32)
            for i in range(total_rows // BLOCK):
                rows = slice(i * BLOCK, (i + 1) * BLOCK)
                one = received[c, rows, :].astype(jnp.float32)
                two = received[c + 2, rows, :].astype(jnp.float32)
                squares = one * one + two * two
                row_scale[rows, :] = squares if c == 0 else row_scale[rows, :] + squares
                even, odd = by_x(one * gain_one, two * gain_two)
                gained_x[2 * pair, rows, lanes] = even
                gained_x[2 * pair + 1, rows, lanes] = odd
    for p in range(n_prompts):
        ranks = slice(p * rank2, (p + 1) * rank2)
        for q in range(quads):
            lanes = slice(q * part, (q + 1) * part)
            for pair in range(2):
                first = total_rows + (q * 4 + pair) * rank2
                second = first + 2 * rank2
                one = received[prompt_slots[p], first : first + rank2, :]
                two = received[prompt_slots[p], second : second + rank2, :]
                even, odd = by_x(one.astype(jnp.float32), two.astype(jnp.float32))
                down_x[2 * pair, ranks, lanes] = even
                down_x[2 * pair + 1, ranks, lanes] = odd
    power = jnp.sum(row_scale[...], axis=1, keepdims=True) * (1.0 / width)
    row_scale[...] = jnp.broadcast_to(lax.rsqrt(power + norm_eps), (total_rows, HEAD_DIM))
    unscaled = jnp.zeros((total_rows, n_prompts * rank2), jnp.float32)
    for x in range(X_SIZE):
        unscaled = unscaled + lax.dot_general(
            gained_x[x], down_x[x], (((1,), (1,)), ((), ())), preferred_element_type=jnp.float32
        )
    lowrank = (unscaled * row_scale[...]).astype(jnp.bfloat16)
    picked = (lowrank.astype(jnp.float32) * in_prompt[...]).astype(jnp.bfloat16)
    update = jnp.dot(picked, up_wide[...], preferred_element_type=jnp.float32)
    offset[:, 0:HEAD_DIM] = bias_wide[0:1] + adapter_scale * update[:, 0:HEAD_DIM]
    offset[:, 2 * HEAD_DIM :] = bias_wide[2:3] + adapter_scale * update[:, HEAD_DIM:]


def block_kernel(
    lengths,
    pages,
    x_place,
    piece_0,
    piece_1,
    piece_2,
    piece_3,
    gained_x,
    row_scale,
    offset,
    cosine,
    sine_part,
    attended,
    cache,
    keys,
    values,
):
    total_rows = gained_x.shape[1]
    inner = gained_x.shape[2]
    blocks = total_rows // QUERY_ROWS
    me = x_place[0]
    unscaled = jnp.zeros(offset.shape, jnp.float32)
    for k, piece in enumerate((piece_0, piece_1, piece_2, piece_3)):
        source = lax.rem(me + (X_SIZE - k), X_SIZE)
        unscaled = unscaled + jnp.dot(
            gained_x[source],
            piece[:, :, 0 : 3 * HEAD_DIM].reshape(inner, 3 * HEAD_DIM),
            preferred_element_type=jnp.float32,
        )
    scale = row_scale[...]
    query_rows = unscaled[:, 0:HEAD_DIM] * scale + offset[:, 0:HEAD_DIM]
    key_rows = unscaled[:, HEAD_DIM : 2 * HEAD_DIM] * scale + offset[:, HEAD_DIM : 2 * HEAD_DIM]
    value_rows = unscaled[:, 2 * HEAD_DIM :] * scale + offset[:, 2 * HEAD_DIM :]
    half = HEAD_DIM // 2
    cos_all = cosine[...]
    sin_all = sine_part[...]
    queries = (query_rows * cos_all + pltpu.roll(query_rows, half, 1) * sin_all).astype(
        jnp.bfloat16
    )
    keys[...] = (key_rows * cos_all + pltpu.roll(key_rows, half, 1) * sin_all).astype(jnp.bfloat16)
    values[...] = value_rows.astype(jnp.bfloat16)
    for page in range(total_rows // PAGE):
        to = pages[0, page]
        cache[to, 0] = keys[page * PAGE : (page + 1) * PAGE, :]
        cache[to, 1] = values[page * PAGE : (page + 1) * PAGE, :]

    end_0 = lengths[0, 0]
    end_1 = end_0 + lengths[0, 1]
    end_2 = end_1 + lengths[0, 2]
    factor = HEAD_DIM ** (-0.5) * LOG2_E
    reach = LONGEST // QUERY_ROWS
    for i in range(blocks):
        low = max(0, i - reach) * QUERY_ROWS
        high = (i + 1) * QUERY_ROWS
        query = queries[i * QUERY_ROWS : high, :]
        scores = lax.dot_general(
            query, keys[low:high, :], (((1,), (1,)), ((), ())), preferred_element_type=jnp.float32
        )
        query_place = i * QUERY_ROWS + lax.broadcasted_iota(jnp.int32, scores.shape, 0)
        key_place = low + lax.broadcasted_iota(jnp.int32, scores.shape, 1)
        start = jnp.where(
            query_place >= end_2,
            end_2,
            jnp.where(query_place >= end_1, end_1, jnp.where(query_place >= end_0, end_0, 0)),
        )
        allowed = (key_place <= query_place) & (key_place >= start)
        scores = jnp.where(allowed, scores, -1e30)
        highest = jnp.max(scores, axis=1, keepdims=True)
        exps = jnp.exp2((scores - highest) * factor)
        total = jnp.sum(exps, axis=1, keepdims=True)
        mixed = jnp.dot(
            exps.astype(jnp.bfloat16), values[low:high, :], preferred_element_type=jnp.float32
        )
        attended[i * QUERY_ROWS : high, :] = (mixed * (1.0 / total)).astype(jnp.bfloat16)


def output_kernel(
    x_place, which, piece_0, piece_1, piece_2, piece_3, attended, out, out_weights, sem
):
    me = x_place[0]
    copies = []
    for k, piece in enumerate((piece_0, piece_1, piece_2, piece_3)):
        source = lax.rem(me + (X_SIZE - k), X_SIZE)
        piece = piece.at[:, :, pl.ds(piece.shape[2] - HEAD_DIM, HEAD_DIM)]
        copies.append(pltpu.make_async_copy(piece, out_weights.at[:, source], sem.at[k]))
        copies[k].start()
    for k in range(X_SIZE):
        copies[k].wait()
    width = out.shape[2]
    weight_out = out_weights[...].reshape(width, HEAD_DIM)
    out_rows = out.shape[1]
    mine = jnp.concatenate(
        [
            attended[pl.ds(pl.multiple_of((2 * y + which[0]) * out_rows, out_rows), out_rows), :]
            for y in range(out.shape[0])
        ],
        axis=0,
    )
    partial = lax.dot_general(
        mine, weight_out, (((1,), (1,)), ((), ())), preferred_element_type=jnp.float32
    )
    out[...] = partial.astype(jnp.bfloat16).reshape(out.shape)


def rotary_tables(rows):
    half = HEAD_DIM // 2
    inverse_freq = np.float32(rope_base) ** (
        -(np.arange(half, dtype=np.float32) * np.float32(2.0) / np.float32(HEAD_DIM))
    )
    angles = (
        np.arange(rows, dtype=np.float32)[:, None] * inverse_freq.astype(np.float32)[None, :]
    ).astype(np.float64)
    cosine = np.concatenate([np.cos(angles)] * 2, axis=1).astype(np.float32)
    sine_part = np.concatenate([np.sin(angles)] * 2, axis=1).astype(np.float32)
    return jnp.asarray(cosine), jnp.asarray(sine_part)


def make_body(n_row, n_col):
    n_z = n_row // X_SIZE
    z_groups = [[z * X_SIZE + x for z in range(n_z)] for x in range(X_SIZE)]
    y_groups = [list(range(core, n_col, 2)) for core in range(2)]

    def x_shift(step):
        return [
            (z * X_SIZE + x, z * X_SIZE + (x + step) % X_SIZE)
            for z in range(n_z)
            for x in range(X_SIZE)
        ]

    def body(
        incoming_hidden,
        input_norm_weight,
        query_key_value_weight,
        query_key_value_bias,
        output_weight,
        adapter_down_weight,
        adapter_up_weight,
        slot_of_adapter,
        adapter_of_prompt,
        prompt_length_list,
        cache_page_index,
    ):
        total_rows, part = incoming_hidden.shape
        rank2 = adapter_down_weight.shape[1] * adapter_down_weight.shape[2]
        width = adapter_down_weight.shape[3]
        row_part = query_key_value_weight.shape[1]
        head_cols = query_key_value_weight.shape[2]
        n_prompts = prompt_length_list.shape[1]
        out_rows = total_rows // n_col
        payload_rows = total_rows + n_col * rank2 + GAIN_ROWS
        payload, weight_copies = pl.pallas_call(
            outgoing_kernel,
            out_shape=(
                jax.ShapeDtypeStruct((payload_rows, part), jnp.bfloat16),
                jax.ShapeDtypeStruct((n_z, row_part, 4 * head_cols), jnp.bfloat16),
            ),
            name="outgoing",
        )(
            incoming_hidden,
            input_norm_weight,
            adapter_down_weight.reshape(rank2, width),
            query_key_value_weight,
            output_weight.T,
        )
        gathered = lax.all_gather(payload, "col", axis=0, tiled=False)
        over_z = lax.all_to_all(weight_copies, "row", 0, 0, tiled=False, axis_index_groups=z_groups)
        own_qkv = over_z[:, :, : 3 * head_cols]
        own_out = over_z[:, :, 3 * head_cols :]
        pieces, out_pieces = [over_z] * X_SIZE, [over_z] * X_SIZE
        for k in (2, 1, 3):
            if k == 2:
                pieces[k] = out_pieces[k] = lax.ppermute(over_z, "row", x_shift(k))
            else:
                pieces[k] = lax.ppermute(own_qkv, "row", x_shift(k))
                out_pieces[k] = lax.ppermute(own_out, "row", x_shift(k))

        cosine, sine_part = rotary_tables(total_rows)
        x_place = lax.rem(lax.axis_index("row"), X_SIZE).astype(jnp.int32).reshape(1)

        whole = pl.BlockSpec(memory_space=VMEM)
        scalar = pl.BlockSpec(memory_space=SMEM)
        raw = pl.BlockSpec(memory_space=pl.ANY)
        gained_x, row_scale, offset, cos_all, sin_all = pl.pallas_call(
            norm_kernel,
            out_shape=(
                jax.ShapeDtypeStruct((X_SIZE, total_rows, width // X_SIZE), jnp.bfloat16),
                jax.ShapeDtypeStruct((total_rows, head_cols), jnp.float32),
                jax.ShapeDtypeStruct((total_rows, 3 * head_cols), jnp.float32),
                jax.ShapeDtypeStruct((total_rows, head_cols), jnp.float32),
                jax.ShapeDtypeStruct((total_rows, head_cols), jnp.float32),
            ),
            in_specs=[scalar] * 3 + [pl.BlockSpec(memory_space=HBM)] + [whole] * 4,
            out_specs=(whole,) * 5,
            scratch_shapes=[
                pltpu.VMEM((n_col, payload_rows, part), jnp.bfloat16),
                pltpu.VMEM((X_SIZE, n_prompts * rank2, width // X_SIZE), jnp.bfloat16),
                pltpu.VMEM((n_prompts * rank2, 2 * head_cols), jnp.bfloat16),
                pltpu.VMEM((total_rows, n_prompts * rank2), jnp.float32),
                pltpu.SemaphoreType.DMA((n_col // 4,)),
            ],
            compiler_params=pltpu.CompilerParams(vmem_limit_bytes=32 * 1024 * 1024),
            name="norm_and_adapters",
        )(
            slot_of_adapter,
            adapter_of_prompt,
            prompt_length_list,
            pltpu.with_memory_space_constraint(gathered, HBM),
            query_key_value_bias,
            adapter_up_weight,
            cosine,
            sine_part,
        )
        attended, cache = pl.pallas_call(
            block_kernel,
            out_shape=(
                jax.ShapeDtypeStruct((total_rows, head_cols), jnp.bfloat16),
                jax.ShapeDtypeStruct((total_rows // PAGE, 2, PAGE, head_cols), jnp.bfloat16),
            ),
            in_specs=[scalar] * 3 + [whole] * 9,
            out_specs=(whole, whole),
            scratch_shapes=[
                pltpu.VMEM((total_rows, head_cols), jnp.bfloat16),
                pltpu.VMEM((total_rows, head_cols), jnp.bfloat16),
            ],
            compiler_params=pltpu.CompilerParams(vmem_limit_bytes=32 * 1024 * 1024),
            name="attention_block",
        )(
            prompt_length_list,
            cache_page_index,
            x_place,
            *pieces,
            gained_x,
            row_scale,
            offset,
            cos_all,
            sin_all,
        )
        core = lax.rem(lax.axis_index("col"), 2).astype(jnp.int32).reshape(1)
        half_shape = jax.ShapeDtypeStruct((n_col // 2, out_rows, width), jnp.bfloat16)
        project = pl.pallas_call(
            output_kernel,
            out_shape=half_shape,
            in_specs=[scalar] * 2 + [raw] * X_SIZE + [whole],
            out_specs=whole,
            scratch_shapes=[
                pltpu.VMEM((n_z, X_SIZE, row_part, head_cols), jnp.bfloat16),
                pltpu.SemaphoreType.DMA((X_SIZE,)),
            ],
            compiler_params=pltpu.CompilerParams(vmem_limit_bytes=32 * 1024 * 1024),
            name="output_projection",
        )
        send = project(x_place, 1 - core, *out_pieces, attended)
        keep = project(x_place, core, *out_pieces, attended)
        received = lax.ppermute(send, "col", [(i, i ^ 1) for i in range(n_col)])
        pair_sum = (keep.astype(jnp.float32) + received.astype(jnp.float32)).astype(jnp.bfloat16)
        terms = lax.all_to_all(pair_sum, "col", 0, 0, tiled=False, axis_index_groups=y_groups)
        summed = jnp.sum(terms.astype(jnp.float32), axis=0).astype(jnp.bfloat16)
        return (summed, cache)

    return body


def solution(mesh):
    in_specs = (
        P("row", "col"),
        P(None, "col"),
        P(None, "row", "col"),
        P(None, "col"),
        P("col", "row"),
        P("col", None, None, None),
        P(None, None, None, "col"),
        P(),
        P("row", None),
        P("row", None),
        P("row", None),
    )
    out_specs = (P(("row", "col"), None), P("row", None, None, "col"))
    body = make_body(mesh.shape["row"], mesh.shape["col"])
    return jax.shard_map(body, mesh=mesh, in_specs=in_specs, out_specs=out_specs, check_vma=False)
```
